256 devices in a mesh: dp: 32 (over y, z), vocab: 8 (over x, core).
Axes of the slice: x: 4, y: 4, z: 8, core: 2. Of those that a mesh axis runs over, the one named last changes fastest.
Arguments:
- hidden: bfloat16 [12288, 4096], P('dp'), may hold values from -6 to 6
- head_weight: bfloat16 [4096, 16000], P('dp', 'vocab'), may hold values from -0.09375 to 0.09375
- head_bias: float32 [16000], P('vocab'), may hold values from -3.5 to -1.5
- query_len: int32 [128], P('dp'), may hold values from 8 to 32
- passage_len: int32 [128], P('dp'), may hold values from 16 to 64
- neg_owner: int32 [128, 8], P('dp'), may hold values from 0 to 31, all different within a row; in each aligned block of 4 rows (0 to 3, 4 to 7, ...) at most 2 rows name the same one
- neg_index: int32 [128, 8], P('dp'), may hold values from 0 to 3
- teacher: float32 [128, 8], P('dp'), may hold values from -8 to 8
Outputs:
- margin_error: float32 [128, 8], P('dp')
- hidden_grad: float32 [12288, 4096], P(('dp', 'vocab'))
The draws below stay inside these ranges and needn't reach their ends.
Inputs may be any that keep to these rules, and one draw needn't show every extreme that they name: `neg_owner`: the 8 negatives of a query have different holders. Among the queries of one index of dp no holder appears more than 2 times, and in some of those blocks one holder appears exactly 2 times.
All inputs are finite; a program needn't handle non-finite values.
Results may differ from the reference program's by a relative error of at most 0.0028.
Values may be sent and summed in bfloat16 or wider, within the bound.
A program may use at most 128 MiB of HBM per device.

```python
import math
import jax
import jax.numpy as jnp
import numpy as np
from jax import lax

D = 4096
VOCAB = 16000
Q_DEV = 4
LQ = 32
LP = 64
NEG = 8
CAP = 2
TOK_DEV = 384
QUERIES = 128
ROWS = 12288
N_DP = 32


def with_ends(result, key, least, largest):
    spot = [jax.random.randint(jax.random.fold_in(key, axis), (), 0, length) for axis, length in enumerate(result.shape)]
    main_axis = result.shape.index(max(result.shape))
    beside = spot[:main_axis] + [(spot[main_axis] + 1) % result.shape[main_axis]] + spot[main_axis + 1:]
    return result.at[tuple(spot)].set(least).at[tuple(beside)].set(largest)


def levels(own_key, dims, shards, least, top_value):
    loudness = 1.0
    for position, shards_of in shards:
        heights = jax.random.uniform(jax.random.fold_in(jax.random.fold_in(own_key, 6), position), (shards_of,), jnp.float32, least / len(shards), top_value / len(shards))
        loudness = loudness * jnp.repeat(jnp.exp(heights), dims[position] // shards_of).reshape((-1,) + (1,) * (len(dims) - 1 - position))
    return loudness


def deal_out(stream_key, own, number, rows, count, top, bound, slope):
    ranking = jax.random.permutation(stream_key, count)
    heavy_load, common = shares(count, rows * top, bound, slope, True), shares(count, rows * top, bound, slope, False)
    places = jnp.arange(count)

    def named(sizes, offset_by):
        used = int((sizes > 0).sum())
        fixed = max(1, used // 4)
        passed = fixed + (places - fixed + offset_by * (used - fixed)) % max(1, count - fixed)
        return jnp.zeros((count,), jnp.int32).at[ranking[jnp.where(places < fixed, places, passed)]].set(jnp.asarray(sizes, jnp.int32))

    sizes = jnp.where(number % 4 == 0, named(heavy_load, number // 4), named(common, number - number // 4 - 1))
    mixed = jax.random.permutation(jax.random.fold_in(own, 3), count)
    giver, taker = mixed[0:count // 2 * 2:2], mixed[1:count // 2 * 2:2]
    room = jnp.minimum(sizes[giver] - 1, bound - sizes[taker]) // 2
    room = jnp.where((giver == ranking[0]) | (taker == ranking[0]) | (sizes[taker] == 0), 0, jnp.maximum(room, 0))
    passed = jax.random.randint(jax.random.fold_in(own, 4), (count // 2,), 0, 1 << 20) % (room + 1)
    sizes = sizes.at[giver].add(-passed).at[taker].add(passed)
    items = jnp.searchsorted(jnp.cumsum(sizes), jnp.arange(rows * top), side="right").astype(jnp.int32)
    listing = items.reshape(top, rows).T
    listing = listing[jax.random.permutation(jax.random.fold_in(own, 1), rows)]
    offset_by = jax.random.randint(jax.random.fold_in(own, 2), (rows, 1), 0, top)
    return jnp.take_along_axis(listing, (jnp.arange(top)[None, :] + offset_by) % top, axis=1)


def shares(amount, total, bound, lean, full):
    portions = [(1 << 20) // math.isqrt(grade ** lean) + 1 for grade in range(1, amount + 1)]
    largest = bound if full else min(bound, max(-(-total // amount), total * portions[0] // sum(portions)))
    least = 1 if total - largest >= amount - 1 else 0
    given, spare = [largest] + [least] * (amount - 1), total - largest - least * (amount - 1)
    while spare > 0:
        movable = [i for i in range(1, amount) if given[i] < largest] or [i for i in range(1, amount) if given[i] < bound]
        mass, remaining = sum([portions[i] for i in movable]), spare
        for i in movable:
            more = min(bound - given[i], max(1, remaining * portions[i] // mass), spare)
            given[i] = given[i] + more
            spare = spare - more
    return np.array(given)


def scatter_about(key, shape, spread, reach, shards=(), dtype=jnp.bfloat16):
    loudness = levels(key, shape, shards, -0.22, 0.18) if shards else 1.0
    drawn = jax.random.normal(key, shape, jnp.float32) * spread * loudness
    return jnp.minimum(jnp.maximum(drawn, -reach), reach).astype(dtype)


def setup_inputs(seed: int = 0) -> dict:
    seeds = jax.random.split(jax.random.key(seed), 9)
    hidden = scatter_about(seeds[0], (ROWS, D), 1.0, 6.0, ((0, 32),))
    head_weight = scatter_about(seeds[1], (D, VOCAB), D ** -0.5, 0.09375, ((0, 32), (1, 8)))
    head_bias = jnp.clip(-3.5 + 2.0 * jax.random.uniform(seeds[2], (VOCAB,), jnp.float32) ** levels(seeds[2], (VOCAB,), ((0, 8),), -0.2, 0.2), -3.5, -1.5)
    query_len = with_ends(jax.random.randint(seeds[3], (QUERIES,), LQ // 4, LQ + 1), jax.random.fold_in(seeds[3], 1), LQ // 4, LQ).astype(jnp.int32)
    passage_len = with_ends(jax.random.randint(seeds[4], (QUERIES,), LP // 4, LP + 1), jax.random.fold_in(seeds[4], 1), LP // 4, LP).astype(jnp.int32)
    neg_owner_keys = jax.random.split(jax.random.fold_in(seeds[5], 1), QUERIES // Q_DEV)
    neg_owner_turns = jax.random.permutation(jax.random.fold_in(seeds[5], 3), QUERIES // Q_DEV)
    neg_owner = jax.vmap(lambda own, number: deal_out(jax.random.fold_in(seeds[5], 2), own, number, Q_DEV, N_DP, NEG, CAP, 2))(neg_owner_keys, neg_owner_turns).reshape((QUERIES, NEG))
    neg_index = with_ends(jax.random.randint(seeds[6], (QUERIES, NEG), 0, Q_DEV), jax.random.fold_in(seeds[6], 1), 0, Q_DEV - 1).astype(jnp.int32)
    teacher = scatter_about(seeds[7], (QUERIES, NEG), 2.0, 8.0, ((0, 32),), jnp.float32)
    return dict(hidden=hidden, head_weight=head_weight, head_bias=head_bias, query_len=query_len, passage_len=passage_len, neg_owner=neg_owner, neg_index=neg_index, teacher=teacher)


TAU = 0.05


def soft_pool(token_logits, token_mask):
    activation = jnp.log1p(jnp.maximum(token_logits, 0.0))
    weights = jnp.exp(activation / TAU) * token_mask[:, :, None]
    summed = jnp.sum(weights, axis=1)
    valid_count = jnp.sum(token_mask, axis=1)[:, None]
    return TAU * jnp.log(summed / valid_count), weights / summed[:, None, :]


def lengths_mask(lengths, span):
    return (jnp.arange(span)[None, :] < lengths[:, None]).astype(jnp.float32)


def block_logits(row_block, head_weight, head_bias):
    return jnp.dot(row_block, head_weight, preferred_element_type=jnp.float32) + head_bias[None, :]


def reference(hidden, head_weight, head_bias, query_len, passage_len, neg_owner, neg_index, teacher):
    blocks = hidden.reshape(N_DP, TOK_DEV, D)
    query_mask = lengths_mask(query_len, LQ).reshape(N_DP, Q_DEV, LQ)
    passage_mask = lengths_mask(passage_len, LP).reshape(N_DP, Q_DEV, LP)
    query_tokens = Q_DEV * LQ

    def forward(items):
        row_block, q_mask, p_mask = items
        logits = block_logits(row_block, head_weight, head_bias)
        query_rep, unused_q = soft_pool(logits[:query_tokens].reshape(Q_DEV, LQ, VOCAB), q_mask)
        passage_rep, unused_p = soft_pool(logits[query_tokens:].reshape(Q_DEV, LP, VOCAB), p_mask)
        return query_rep, passage_rep

    query_rep, passage_rep = lax.map(forward, (blocks, query_mask, passage_mask))
    query_rep = query_rep.reshape(QUERIES, VOCAB)
    passage_rep = passage_rep.reshape(QUERIES, VOCAB)
    passage_ids = (neg_owner * Q_DEV + neg_index).astype(jnp.int32)
    positive = jnp.sum(query_rep * passage_rep, axis=1)
    neg_rows = passage_rep[passage_ids]
    negative = jnp.sum(query_rep[:, None, :] * neg_rows, axis=2)
    margin_error = positive[:, None] - negative - teacher
    grad_pos = jnp.sum(margin_error, axis=1)
    grad_neg = -margin_error
    query_grad = grad_pos[:, None] * passage_rep + jnp.sum(grad_neg[:, :, None] * neg_rows, axis=1)
    neg_terms = (grad_neg[:, :, None] * query_rep[:, None, :]).reshape(-1, VOCAB)
    passage_grad = grad_pos[:, None] * query_rep + jax.ops.segment_sum(neg_terms, passage_ids.reshape(-1), num_segments=QUERIES)

    def backward(items):
        row_block, q_mask, p_mask, q_grad, p_grad = items
        logits = block_logits(row_block, head_weight, head_bias)
        unused_q, query_weights = soft_pool(logits[:query_tokens].reshape(Q_DEV, LQ, VOCAB), q_mask)
        unused_p, passage_weights = soft_pool(logits[query_tokens:].reshape(Q_DEV, LP, VOCAB), p_mask)
        relu_slope = (logits > 0).astype(jnp.float32) / (1.0 + jnp.maximum(logits, 0.0))
        d_query = (q_grad[:, None, :] * query_weights).reshape(-1, VOCAB)
        d_passage = (p_grad[:, None, :] * passage_weights).reshape(-1, VOCAB)
        logit_grad = (jnp.concatenate([d_query, d_passage], axis=0) * relu_slope).astype(jnp.bfloat16)
        return lax.dot_general(logit_grad, head_weight, (((1,), (1,)), ((), ())), preferred_element_type=jnp.float32)

    grads = lax.map(backward, (blocks, query_mask, passage_mask, query_grad.reshape(N_DP, Q_DEV, VOCAB), passage_grad.reshape(N_DP, Q_DEV, VOCAB)))
    return margin_error, grads.reshape(ROWS, D)
```

```python
import functools

import jax
import jax.numpy as jnp
from jax import lax
from jax.experimental import pallas as pl
from jax.experimental.pallas import tpu as pltpu
from jax.sharding import PartitionSpec as P

NY, NZ, NX = 4, 8, 4
NDP = NY * NZ
LQ, LP, QD, NEG = 32, 64, 4, 8
TOK = QD * (LQ + LP)
D = 4096
KB = D // NDP
VW = 2000
VP = 2048
STREAMS = 4
CW = VP // STREAMS
SUB = 2
SR = KB // SUB
META = VP
RW = VP + 128
CH = 512
NCH = D // CH
ROWS = TOK // 8
SCALE = 2.0**-64
TAU = 0.05
HI = lax.Precision.HIGHEST


def kernel(
    w_hbm, hid_hbm, bias_ref, lens_ref, meta_ref,
    margin_ref, out_ref,
    wf, hid, lg_f, rall, inv_ref, lgrad, sbuf, mt_ref, psum_part, ron, fs, fr, ns, nr,
    ld_sem, rsend, rrecv, zsend, zrecv, ysend, yrecv, vsend, vrecv, osend, orecv, fsend, frecv, nsend, nrecv,
):
    dp = lax.axis_index("dp")
    v = lax.axis_index("vocab")
    y, z = dp // NZ, dp % NZ
    x, c = v // 2, v % 2
    y_up, y_dn = (y + 1) % NY, (y + NY - 1) % NY
    z_up, z_dn = (z + 1) % NZ, (z + NZ - 1) % NZ
    x_up, x_dn, x_far = (x + 1) % NX, (x + NX - 1) % NX, (x + 2) % NX

    def dp_dev(yy, zz):
        return {"dp": yy * NZ + zz}

    def v_dev(xx, cc):
        return {"vocab": xx * 2 + cc}

    def remote(src, dst, ss, rs, dev):
        return pltpu.make_async_remote_copy(
            src_ref=src, dst_ref=dst, send_sem=ss, recv_sem=rs, device_id=dev,
            device_id_type=pl.DeviceIdType.MESH,
        )

    my_rows = pl.ds(pl.multiple_of(dp * KB, KB), KB)
    ld_w = pltpu.make_async_copy(w_hbm, wf.at[my_rows, :], ld_sem.at[0])
    ld_h = pltpu.make_async_copy(hid_hbm, hid, ld_sem.at[1])
    ld_w.start()
    ld_h.start()

    barrier = pltpu.get_barrier_semaphore()
    peers = [dp_dev(y_up, z), dp_dev(y_dn, z), dp_dev(y, z_up), dp_dev(y, z_dn)]
    peers += [{"vocab": (v + i) % (2 * NX)} for i in range(1, 2 * NX)]
    for dev in peers:
        pl.semaphore_signal(barrier, inc=1, device_id=dev, device_id_type=pl.DeviceIdType.MESH)
    ld_w.wait()
    pl.semaphore_wait(barrier, len(peers))

    pos_a = NY * z + (y + z) % NY
    tb = (z + NY * NZ - (NY - 1) * y) % NZ
    pos_b = NY * (y + NY * (tb // NY)) + tb % NY

    def at_a(p):
        b, i = p // NY, p % NY
        return ((i + NY * NZ - b) % NY) * NZ + b

    def at_b(p):
        b, i = p // NY, p % NY
        return (b % NY) * NZ + ((NY - 1) * b + i) % NZ

    pos, at = (pos_a, pos_a, pos_b, pos_b), (at_a, at_a, at_b, at_b)
    sign = (1, -1, 1, -1)
    nxt = [{"dp": at[q]((pos[q] + NDP + sign[q]) % NDP)} for q in range(STREAMS)]

    def origin(q, s):
        return at[q]((pos[q] + 2 * NDP - sign[q] * s) % NDP)

    def ring_copy(q, s, sub):
        rows = pl.ds(pl.multiple_of(origin(q, s) * KB + sub * SR, SR), SR)
        part = wf.at[rows, pl.ds(q * CW, CW)]
        return remote(part, part, rsend.at[q, s, sub], rrecv.at[q, s, sub], nxt[q])

    def arrived(q, s, sub):
        rows = pl.ds(pl.multiple_of(origin(q, s) * KB + sub * SR, SR), SR)
        part = wf.at[rows, pl.ds(q * CW, CW)]
        remote(part, part, rsend.at[q, s - 1, sub], rrecv.at[q, s - 1, sub], nxt[q]).wait_recv()

    for sub in range(SUB):
        for q in range(STREAMS):
            ring_copy(q, 0, sub).start()
    lg_f[...] = jnp.broadcast_to(bias_ref[...], (TOK, VP))
    rall[z, y, :, META:] = meta_ref[...]
    ld_h.wait()

    def mm(q, s1, s2):
        o1 = pl.multiple_of(origin(q, s1) * KB, KB)
        o2 = pl.multiple_of(origin(q, s2) * KB, KB)
        cols = pl.ds(q * CW, CW)
        rhs = jnp.concatenate([wf[pl.ds(o1, KB), cols], wf[pl.ds(o2, KB), cols]], axis=0)
        lhs = jnp.concatenate([hid[:, pl.ds(o1, KB)], hid[:, pl.ds(o2, KB)]], axis=1)
        lg_f[:, cols] += jnp.dot(lhs, rhs, preferred_element_type=jnp.float32)

    def pass_on(s):
        for sub in range(SUB):
            for q in range(STREAMS):
                arrived(q, s, sub)
                ring_copy(q, s, sub).start()

    def ring_body(t, carry):
        pass_on(2 * t + 1)

        @pl.when(t > 0)
        def _():
            mm(0, 2 * t - 1, 2 * t)
            mm(1, 2 * t - 1, 2 * t)

        pass_on(2 * t + 2)

        @pl.when(t > 0)
        def _():
            mm(2, 2 * t - 1, 2 * t)
            mm(3, 2 * t - 1, 2 * t)

        return carry

    lax.fori_loop(0, (NDP - 2) // 2, ring_body, 0)
    for q in range(STREAMS):
        mm(q, NDP - 3, NDP - 2)
    for q in range(STREAMS):
        for sub in range(SUB):
            arrived(q, NDP - 1, sub)
        mm(q, 0, NDP - 1)

    row0 = 0
    for g in range(2 * QD):
        span = LQ if g < QD else LP
        n = lens_ref[g]
        mask = lax.broadcasted_iota(jnp.int32, (span, CW), 0) < n
        count = n.astype(jnp.float32)
        for q in range(STREAMS):
            cols = slice(q * CW, (q + 1) * CW)
            l = lg_f[row0 : row0 + span, cols]
            u = 1.0 + jnp.maximum(l, 0.0)
            u2 = u * u
            u4 = u2 * u2
            u8 = u4 * u4
            u16 = u8 * u8
            u19 = jnp.where(mask, u16 * (u2 * u), 0.0)
            summed = jnp.sum(u19 * u, axis=0, keepdims=True)
            lg_f[row0 : row0 + span, cols] = jnp.where(l > 0.0, u19 * SCALE, 0.0)
            rall[z, y, g : g + 1, cols] = TAU * jnp.log(summed / count)
            inv_ref[g : g + 1, cols] = 1.0 / (summed * SCALE)
        row0 += span

    half = VP // 2
    h1 = pl.ds(0, half)
    h0 = pl.ds(half, RW - half)
    far1 = (pl.ds(0, half // 2), pl.ds(half // 2, half // 2))
    far0 = (pl.ds(half, 512), pl.ds(half + 512, RW - half - 512))
    sends = []

    def go(src, ss, rs, dev):
        cp = remote(src, src, ss, rs, dev)
        cp.start()
        sends.append(cp)

    z_next = (dp_dev(y, z_up), dp_dev(y, z_dn))

    def z_origin(way, d):
        return (z + NZ - d) % NZ if way == 0 else (z + d) % NZ

    def z_ref(kind, way, d):
        zo = z_origin(way, d)
        if kind == 0:
            cols = far0[way] if d == NZ // 2 else h0
            return rall.at[zo, :, :, cols]
        cols = far1[way] if d == NZ // 2 else h1
        return rall.at[zo, y, :, cols]

    def z_send(kind, way, d):
        zo = z_origin(way, d - 1)
        if kind == 0:
            cols = far0[way] if d == NZ // 2 else h0
            src = rall.at[zo, :, :, cols]
        else:
            cols = far1[way] if d == NZ // 2 else h1
            src = rall.at[zo, y, :, cols]
        go(src, zsend.at[kind, way, d - 1], zrecv.at[kind, way, d - 1], z_next[way])

    def z_wait(kind, way, d):
        ref = z_ref(kind, way, d)
        remote(ref, ref, zsend.at[kind, way, d - 1], zrecv.at[kind, way, d - 1], z_next[way]).wait_recv()

    def y_send(slot, zo, cols):
        go(rall.at[zo, y, :, cols], ysend.at[slot, 0], yrecv.at[slot, 0], dp_dev(y_up, z))
        go(rall.at[zo, y, :, cols], ysend.at[slot, 1], yrecv.at[slot, 1], dp_dev(y_dn, z))

    def y_wait(slot, way, zo, cols):
        yo = (y_dn, y_up, (y + 2) % NY)[way]
        ref = rall.at[zo, yo, :, cols]
        remote(ref, ref, ysend.at[slot, way], yrecv.at[slot, way], dp_dev(y_up, z)).wait_recv()

    def y_relay(slot, zo, cols):
        y_wait(slot, 0, zo, cols)
        y_wait(slot, 1, zo, cols)
        odd = zo % 2
        src_y = (y + NY - 1 + 2 * odd) % NY
        dst_y = (y + 1 + 2 * odd) % NY
        go(rall.at[zo, src_y, :, cols], ysend.at[slot, 2], yrecv.at[slot, 2], dp_dev(dst_y, z))

    y_send(NZ, z, h0)
    z_send(1, 0, 1)
    z_send(1, 1, 1)
    y_send(0, z, h1)
    y_relay(NZ, z, h0)
    y_wait(NZ, 2, z, h0)
    z_send(0, 0, 1)
    z_send(0, 1, 1)
    y_relay(0, z, h1)
    order = [(0, z)]
    last = []
    for d in range(1, NZ // 2 + 1):
        fresh = []
        for way in range(2):
            z_wait(1, way, d)
            if d < NZ // 2:
                z_send(1, way, d + 1)
                slot = 2 * d - 1 + way
                y_send(slot, z_origin(way, d), h1)
                fresh.append((slot, z_origin(way, d)))
        if d == NZ // 2:
            y_send(NZ - 1, z_origin(0, d), h1)
            fresh.append((NZ - 1, z_origin(0, d)))
        for way in range(2):
            z_wait(0, way, d)
            if d < NZ // 2:
                z_send(0, way, d + 1)
        for slot, zo in last:
            y_relay(slot, zo, h1)
        last = fresh
        order += fresh
    for slot, zo in last:
        y_relay(slot, zo, h1)
    for slot, zo in order:
        y_wait(slot, 2, zo, h1)

    n_rows = NDP * 8
    reps = rall[:, :, :, 0:VP].reshape(n_rows, VP)
    gram = lax.dot_general(
        reps, reps, (((1,), (1,)), ((), ())), precision=HI, preferred_element_type=jnp.float32
    )
    meta = rall[:, :, :, META:].reshape(n_rows, 128)
    meta_t = meta.T
    row_id = lax.broadcasted_iota(jnp.int32, (n_rows, n_rows), 0).astype(jnp.float32)
    lane_id = lax.broadcasted_iota(jnp.int32, (n_rows, n_rows), 1).astype(jnp.float32)
    for k in range(NEG):
        hit = row_id == meta_t[k : k + 1, :]
        sbuf[v, k : k + 1, :] = jnp.sum(jnp.where(hit, gram, 0.0), axis=0, keepdims=True)
    is_pos = row_id == lane_id + QD
    sbuf[v, NEG : NEG + 1, :] = jnp.sum(jnp.where(is_pos, gram, 0.0), axis=0, keepdims=True)
    sbuf[v, NEG + 1 :, :] = jnp.zeros((16 - NEG - 1, n_rows), jnp.float32)
    for i in range(1, 2 * NX):
        go(sbuf.at[v], vsend.at[i - 1], vrecv.at[i - 1], {"vocab": (v + i) % (2 * NX)})
    for i in range(1, 2 * NX):
        ref = sbuf.at[(v + 2 * NX - i) % (2 * NX)]
        remote(ref, ref, vsend.at[i - 1], vrecv.at[i - 1], {"vocab": (v + i) % (2 * NX)}).wait_recv()
    total = sbuf[0]
    for i in range(1, 2 * NX):
        total = total + sbuf[i]
    lane8 = lax.broadcasted_iota(jnp.int32, (NEG, n_rows), 1)
    margin = total[NEG : NEG + 1, :] - total[0:NEG, :] - meta_t[NEG : 2 * NEG, :]
    margin = jnp.where(lane8 % 8 < QD, margin, 0.0)
    mt_ref[...] = jnp.concatenate([margin, jnp.zeros((120, n_rows), jnp.float32)], axis=0).T
    base = pl.multiple_of((z * NY + y) * 8, 8)
    m_loc = mt_ref[pl.ds(base, 8), :]
    margin_ref[...] = m_loc[0:QD, 0:NEG]

    meta_loc = rall[z, y, :, META:]
    sub_id = (lax.broadcasted_iota(jnp.int32, (8, n_rows), 0) + base).astype(jnp.float32)
    lanes = lax.broadcasted_iota(jnp.int32, (8, n_rows), 1).astype(jnp.float32)
    grad_pos_t = jnp.sum(margin, axis=0, keepdims=True)
    grad_pos_l = jnp.sum(m_loc[:, 0:NEG], axis=1, keepdims=True)
    coef = jnp.where(sub_id == lanes + QD, grad_pos_t, 0.0)
    coef = coef + jnp.where(lanes == sub_id + QD, grad_pos_l, 0.0)
    for k in range(NEG):
        coef = coef - jnp.where(sub_id == meta_t[k : k + 1, :], margin[k : k + 1, :], 0.0)
        coef = coef - jnp.where(lanes == meta_loc[:, k : k + 1], m_loc[:, k : k + 1], 0.0)
    rep_grad = lax.dot_general(
        coef, reps, (((1,), (0,)), ((), ())), precision=HI, preferred_element_type=jnp.float32
    )
    row0 = 0
    for g in range(2 * QD):
        span = LQ if g < QD else LP
        e = lg_f[row0 : row0 + span, :]
        lgrad[row0 : row0 + span, :] = ((e * inv_ref[g : g + 1, :]) * rep_grad[g : g + 1, :]).astype(jnp.bfloat16)
        row0 += span

    other = 1 - c

    def on_copy(n):
        return remote(psum_part.at[n, other], ron.at[n], osend.at[n], orecv.at[n], v_dev(x, other))

    def far_copy(n, way):
        return remote(
            fs.at[n, way], fr.at[n, way], fsend.at[n, way], frecv.at[n, way], v_dev((x_up, x_dn)[way], c)
        )

    def near_copy(n, way):
        return remote(
            ns.at[n, way], nr.at[n, way], nsend.at[n, way], nrecv.at[n, way], v_dev((x_up, x_dn)[way], c)
        )

    hw = CH // 2

    def bwd_body(n, carry):
        @pl.when(n < NCH)
        def _():
            rows = pl.ds(pl.multiple_of(n * CH, CH), CH)
            res = lax.dot_general(
                lgrad[...], wf[rows, :], (((1,), (1,)), ((), ())), preferred_element_type=jnp.float32
            )
            for i in range(2 * NX):
                psum_part[n, i % 2, i // 2] = res[i * ROWS : (i + 1) * ROWS, :]
            on_copy(n).start()

        @pl.when((n >= 1) & (n < NCH + 1))
        def _():
            m = n - 1
            on_copy(m).wait_recv()
            far = psum_part[m, c, x_far] + ron[m, x_far]
            fs[m, 0] = far[:, :hw].astype(jnp.bfloat16)
            fs[m, 1] = far[:, hw:].astype(jnp.bfloat16)
            far_copy(m, 0).start()
            far_copy(m, 1).start()

        @pl.when((n >= 2) & (n < NCH + 2))
        def _():
            m = n - 2
            up = psum_part[m, c, x_up] + ron[m, x_up]
            dn = psum_part[m, c, x_dn] + ron[m, x_dn]
            far_copy(m, 0).wait_recv()
            far_copy(m, 1).wait_recv()
            ns[m, 0, :, :hw] = (up[:, :hw] + fr[m, 0].astype(jnp.float32)).astype(jnp.bfloat16)
            ns[m, 0, :, hw:] = up[:, hw:].astype(jnp.bfloat16)
            ns[m, 1, :, :hw] = dn[:, :hw].astype(jnp.bfloat16)
            ns[m, 1, :, hw:] = (dn[:, hw:] + fr[m, 1].astype(jnp.float32)).astype(jnp.bfloat16)
            near_copy(m, 0).start()
            near_copy(m, 1).start()

        @pl.when(n >= 3)
        def _():
            m = n - 3
            own = psum_part[m, c, x] + ron[m, x]
            near_copy(m, 0).wait_recv()
            near_copy(m, 1).wait_recv()
            cols = pl.ds(pl.multiple_of(m * CH, CH), CH)
            out_ref[:, cols] = own + nr[m, 0].astype(jnp.float32) + nr[m, 1].astype(jnp.float32)

        return carry

    lax.fori_loop(0, NCH + 3, bwd_body, 0)

    for cp in sends:
        cp.wait_send()

    def drain(s, carry):
        for q in range(STREAMS):
            for sub in range(SUB):
                ring_copy(q, s, sub).wait_send()
        return carry

    lax.fori_loop(0, NDP - 1, drain, 0)
    for n in range(NCH):
        on_copy(n).wait_send()
        for way in range(2):
            far_copy(n, way).wait_send()
            near_copy(n, way).wait_send()


def per_device(
    hidden, head_weight, head_bias, query_len, passage_len, neg_owner, neg_index, teacher
):
    w = jnp.pad(head_weight, ((0, 0), (0, VP - VW)))
    bias = jnp.pad(head_bias, (0, VP - VW))[None, :]
    lens = jnp.concatenate([query_len, passage_len])
    ids = ((neg_owner % NZ) * NY + neg_owner // NZ) * 8 + QD + neg_index
    meta = jnp.concatenate([ids.astype(jnp.float32), teacher], axis=1)
    meta = jnp.pad(meta, ((0, 4), (0, 112)), constant_values=-1.0)
    dma = pltpu.SemaphoreType.DMA
    vm = pltpu.VMEM
    f32, bf16 = jnp.float32, jnp.bfloat16
    margin, grad = pl.pallas_call(
        kernel,
        out_shape=(
            jax.ShapeDtypeStruct((QD, NEG), f32),
            jax.ShapeDtypeStruct((ROWS, D), f32),
        ),
        in_specs=[
            pl.BlockSpec(memory_space=pl.ANY),
            pl.BlockSpec(memory_space=pl.ANY),
            pl.BlockSpec(memory_space=pltpu.VMEM),
            pl.BlockSpec(memory_space=pltpu.SMEM),
            pl.BlockSpec(memory_space=pltpu.VMEM),
        ],
        out_specs=(pl.BlockSpec(memory_space=pltpu.VMEM), pl.BlockSpec(memory_space=pltpu.VMEM)),
        scratch_shapes=[
            vm((D, VP), bf16),
            vm((TOK, D), bf16),
            vm((TOK, VP), f32),
            vm((NZ, NY, 8, RW), f32),
            vm((8, VP), f32),
            vm((TOK, VP), bf16),
            vm((2 * NX, 16, NDP * 8), f32),
            vm((NDP * 8, 128), f32),
            vm((NCH, 2, NX, ROWS, CH), f32),
            vm((NCH, NX, ROWS, CH), f32),
            vm((NCH, 2, ROWS, CH // 2), bf16),
            vm((NCH, 2, ROWS, CH // 2), bf16),
            vm((NCH, 2, ROWS, CH), bf16),
            vm((NCH, 2, ROWS, CH), bf16),
            dma((2,)),
            dma((STREAMS, NDP, SUB)),
            dma((STREAMS, NDP, SUB)),
            dma((2, 2, NZ // 2)),
            dma((2, 2, NZ // 2)),
            dma((NZ + 1, 3)),
            dma((NZ + 1, 3)),
            dma((2 * NX - 1,)),
            dma((2 * NX - 1,)),
            dma((NCH,)),
            dma((NCH,)),
            dma((NCH, 2)),
            dma((NCH, 2)),
            dma((NCH, 2)),
            dma((NCH, 2)),
        ],
        compiler_params=pltpu.CompilerParams(
            collective_id=0, has_side_effects=True, vmem_limit_bytes=60 * 1024 * 1024
        ),
    )(w, hidden, bias, lens, meta)
    return margin, grad


def solution(mesh):
    return jax.shard_map(
        per_device,
        mesh=mesh,
        in_specs=(
            P("dp", None),
            P("dp", "vocab"),
            P("vocab"),
            P("dp"),
            P("dp"),
            P("dp", None),
            P("dp", None),
            P("dp", None),
        ),
        out_specs=(P("dp", None), P(("dp", "vocab"), None)),
        check_vma=False,
    )
```

```python
import functools

import jax
import jax.numpy as jnp
from jax import lax
from jax.experimental import pallas as pl
from jax.experimental.pallas import tpu as pltpu
from jax.sharding import PartitionSpec as P

NY, NZ, NX = 4, 8, 4
NDP = NY * NZ
LQ, LP, QD, NEG = 32, 64, 4, 8
TOK = QD * (LQ + LP)
D = 4096
KB = D // NDP
VW = 2000
VP = 2048
STREAMS = 4
CW = VP // STREAMS
HW = VP // 2
SUB = 4
SR = HW // SUB
FAR = NDP // 2
META = VP
RW = VP + 128
CH = 512
NCH = D // CH
S2, S3, S4 = 2, 5, 8
ROWS = TOK // 8
SCALE = 2.0**-64
TAU = 0.05
HI = lax.Precision.HIGHEST


def rem(a, n):
    return lax.rem(a, jnp.int32(n))


def div(a, n):
    return lax.div(a, jnp.int32(n))


def kernel(
    w_hbm, hid_hbm, bias_ref, qlen_ref, plen_ref, owner_ref, index_ref, teacher_ref,
    margin_ref, out_ref,
    wt, hid, bias_s, lg_f, rall, inv_ref, lgrad, sbuf, mt_ref, psum_part, ron, fs, fr, ns, nr,
    ld_sem, rsend, rrecv, zsend, zrecv, ysend, yrecv, vsend, vrecv, osend, orecv, fsend, frecv, nsend, nrecv,
):
    dp = lax.axis_index("dp")
    v = lax.axis_index("vocab")
    y, z = div(dp, NZ), rem(dp, NZ)
    x, c = div(v, 2), rem(v, 2)
    y_up, y_dn = rem(y + 1, NY), rem(y + NY - 1, NY)
    z_up, z_dn = rem(z + 1, NZ), rem(z + NZ - 1, NZ)
    x_up, x_dn, x_far = rem(x + 1, NX), rem(x + NX - 1, NX), rem(x + 2, NX)

    def dp_dev(yy, zz):
        return {"dp": yy * NZ + zz}

    def v_dev(xx, cc):
        return {"vocab": xx * 2 + cc}

    def remote(src, dst, ss, rs, dev):
        return pltpu.make_async_remote_copy(
            src_ref=src, dst_ref=dst, send_sem=ss, recv_sem=rs, device_id=dev,
            device_id_type=pl.DeviceIdType.MESH,
        )

    ld_w = pltpu.make_async_copy(w_hbm, wt.at[dp, 0:VW, :], ld_sem.at[0])
    ld_h = pltpu.make_async_copy(hid_hbm, hid, ld_sem.at[1])
    ld_w.start()
    ld_h.start()

    barrier = pltpu.get_barrier_semaphore()
    peers = [dp_dev(y_up, z), dp_dev(y_dn, z), dp_dev(y, z_up), dp_dev(y, z_dn)]
    peers += [{"vocab": rem(v + i, 2 * NX)} for i in range(1, 2 * NX)]
    for dev in peers:
        pl.semaphore_signal(barrier, inc=1, device_id=dev, device_id_type=pl.DeviceIdType.MESH)
    ld_w.wait()
    pl.semaphore_wait(barrier, len(peers))

    pos_a = NY * z + rem(y + z, NY)
    tb = rem(z + NY * NZ - (NY - 1) * y, NZ)
    pos_b = NY * (y + NY * div(tb, NY)) + rem(tb, NY)

    def at_a(p):
        b, i = div(p, NY), rem(p, NY)
        return rem(i + NY * NZ - b, NY) * NZ + b

    def at_b(p):
        b, i = div(p, NY), rem(p, NY)
        return rem(b, NY) * NZ + rem((NY - 1) * b + i, NZ)

    pos, at = (pos_a, pos_a, pos_b, pos_b), (at_a, at_a, at_b, at_b)
    sign = (1, -1, 1, -1)
    nxt = [{"dp": at[q](rem(pos[q] + NDP + sign[q], NDP))} for q in range(STREAMS)]

    def origin(q, s):
        return at[q](rem(pos[q] + 2 * NDP - sign[q] * s, NDP))

    def ring_copy(q, org, s, sub):
        part = wt.at[org, pl.ds((q // 2) * HW + sub * SR, sub_rows(q, sub)), :]
        return remote(part, part, rsend.at[q, sub], rrecv.at[q, s, sub], nxt[q])

    def sub_rows(q, sub):
        return SR if q < 2 or sub < SUB - 1 else VW - (VP - SR)

    def far_subs(q):
        return range(0, SUB // 2) if q % 2 == 0 else range(SUB // 2, SUB)

    for sub in range(SUB):
        for q in range(STREAMS):
            ring_copy(q, dp, 0, sub).start()

    def clear(i, carry):
        wt[i, VW:, :] = jnp.zeros((VP - VW, KB), jnp.bfloat16)
        return carry

    lax.fori_loop(0, NDP, clear, 0)
    bias_s[...] = jnp.zeros_like(bias_s)
    bias_s[:, 0:VW] = bias_ref[...]
    lg_f[...] = jnp.broadcast_to(bias_s[...], (TOK, VP))
    owner = owner_ref[...]
    ids = (rem(owner, NZ) * NY + div(owner, NZ)) * 8 + QD + index_ref[...]
    rall[z, y, :, META:] = jnp.zeros((8, 128), jnp.float32)
    rall[z, y, 0:QD, META : META + NEG] = ids.astype(jnp.float32)
    rall[z, y, QD:8, META : META + NEG] = teacher_ref[...]
    ld_h.wait()

    def mm(q, o1, o2):
        cols = slice(q * CW, (q + 1) * CW)
        k1 = pl.ds(pl.multiple_of(o1 * KB, KB), KB)
        k2 = pl.ds(pl.multiple_of(o2 * KB, KB), KB)
        rhs = jnp.concatenate([wt[o1, cols, :], wt[o2, cols, :]], axis=1)
        lhs = jnp.concatenate([hid[:, k1], hid[:, k2]], axis=1)
        lg_f[:, cols] += lax.dot_general(
            lhs, rhs, (((1,), (1,)), ((), ())), preferred_element_type=jnp.float32
        )

    def mm_after(sub, org):
        mm(sub, org[sub // 2 * 2], org[sub // 2 * 2 + 1])

    def ring_body(s, before):
        org = [origin(q, s) for q in range(STREAMS)]
        for sub in range(SUB):
            for q in range(STREAMS):
                ring_copy(q, org[q], s - 1, sub).wait_recv()
                if sub in far_subs(q):
                    ring_copy(q, org[q], s, sub).start()
                else:

                    @pl.when(s < FAR - 1)
                    def _():
                        ring_copy(q, org[q], s, sub).start()

            @pl.when(s > 1)
            def _():
                mm_after(sub, before)

        return tuple(org)

    before = lax.fori_loop(1, FAR, ring_body, (dp,) * STREAMS)
    for sub in range(SUB):
        mm_after(sub, before)
    for q in range(STREAMS):
        for sub in far_subs(q):
            ring_copy(q, origin(q, FAR), FAR - 1, sub).wait_recv()
    for q in range(STREAMS):
        mm(q, dp, origin(q // 2 * 2, FAR))

    row0 = 0
    for g in range(2 * QD):
        span = LQ if g < QD else LP
        n = qlen_ref[g] if g < QD else plen_ref[g - QD]
        mask = lax.broadcasted_iota(jnp.int32, (span, CW), 0) < n
        count = n.astype(jnp.float32)
        for q in range(STREAMS):
            cols = slice(q * CW, (q + 1) * CW)
            l = lg_f[row0 : row0 + span, cols]
            u = 1.0 + jnp.maximum(l, 0.0)
            u2 = u * u
            u4 = u2 * u2
            u8 = u4 * u4
            u16 = u8 * u8
            u19 = jnp.where(mask, u16 * (u2 * u), 0.0)
            summed = jnp.sum(u19 * u, axis=0, keepdims=True)
            lg_f[row0 : row0 + span, cols] = jnp.where(l > 0.0, u19 * SCALE, 0.0)
            rall[z, y, g : g + 1, cols] = TAU * jnp.log(summed / count)
            inv_ref[g : g + 1, cols] = 1.0 / (summed * SCALE)
        row0 += span

    half = 1280
    h1 = pl.ds(0, half)
    h0 = pl.ds(half, RW - half)
    far1 = (pl.ds(0, 640), pl.ds(640, half - 640))
    far0 = (pl.ds(half, 384), pl.ds(half + 384, RW - half - 384))
    sends = []

    def go(src, ss, rs, dev):
        cp = remote(src, src, ss, rs, dev)
        cp.start()
        sends.append(cp)

    z_next = (dp_dev(y, z_up), dp_dev(y, z_dn))
    y_off = [y, y_dn, y_up, rem(y + 2, NY)]
    mid = NZ // 2

    def z_origin(way, d):
        return rem(z + NZ - d, NZ) if way == 0 else rem(z + d, NZ)

    def z_copy(j, way, d, zo):
        if j < NY:
            ref = rall.at[zo, y_off[j], :, far0[way] if d == mid else h0]
        else:
            ref = rall.at[zo, y, :, far1[way] if d == mid else h1]
        return remote(ref, ref, zsend.at[j, way, d - 1], zrecv.at[j, way, d - 1], z_next[way])

    def z_send(j, way, d):
        cp = z_copy(j, way, d, z_origin(way, d - 1))
        cp.start()
        sends.append(cp)

    def z_wait(j, way, d):
        z_copy(j, way, d, z_origin(way, d)).wait_recv()

    def y_send(slot, zo, cols):
        go(rall.at[zo, y, :, cols], ysend.at[slot, 0], yrecv.at[slot, 0], dp_dev(y_up, z))
        go(rall.at[zo, y, :, cols], ysend.at[slot, 1], yrecv.at[slot, 1], dp_dev(y_dn, z))

    def y_wait(slot, way, zo, cols):
        ref = rall.at[zo, y_off[way + 1], :, cols]
        remote(ref, ref, ysend.at[slot, way], yrecv.at[slot, way], dp_dev(y_up, z)).wait_recv()

    def y_relay(slot, zo, cols):
        y_wait(slot, 0, zo, cols)
        y_wait(slot, 1, zo, cols)
        odd = rem(zo, 2)
        src_y = rem(y + NY - 1 + 2 * odd, NY)
        dst_y = rem(y + 1 + 2 * odd, NY)
        go(rall.at[zo, src_y, :, cols], ysend.at[slot, 2], yrecv.at[slot, 2], dp_dev(dst_y, z))

    y_send(NZ, z, h0)
    for way in range(2):
        z_send(0, way, 1)
        z_send(NY, way, 1)
    y_send(0, z, h1)
    y_relay(NZ, z, h0)
    for way in range(2):
        z_send(1, way, 1)
        z_send(2, way, 1)
    y_wait(NZ, 2, z, h0)
    for way in range(2):
        z_send(3, way, 1)
    last = [(0, z)]
    order = [(0, z)]
    for d in range(1, mid + 1):
        fresh = []
        for j in (0, NY, 1, 2, 3):
            for way in range(2):
                z_wait(j, way, d)
                if d < mid:
                    z_send(j, way, d + 1)
                if j == NY and (d < mid or way == 1):
                    slot = 2 * d - 1 + way if d < mid else NZ - 1
                    y_send(slot, z_origin(way, d), h1)
                    fresh.append((slot, z_origin(way, d)))
            if j == 1:
                for slot, zo in last:
                    y_relay(slot, zo, h1)
        last = fresh
        order += fresh
    for slot, zo in last:
        y_relay(slot, zo, h1)
    for slot, zo in order:
        y_wait(slot, 2, zo, h1)

    n_rows = NDP * 8
    reps = rall[:, :, :, 0:VP].reshape(n_rows, VP)
    gram = lax.dot_general(
        reps, reps, (((1,), (1,)), ((), ())), precision=HI, preferred_element_type=jnp.float32
    )
    meta = rall[:, :, :, META:].reshape(n_rows, 128)
    meta_t = meta.T
    row_id = lax.broadcasted_iota(jnp.int32, (n_rows, n_rows), 0).astype(jnp.float32)
    lane_id = lax.broadcasted_iota(jnp.int32, (n_rows, n_rows), 1).astype(jnp.float32)
    for k in range(NEG):
        hit = row_id == meta_t[k : k + 1, :]
        sbuf[v, k : k + 1, :] = jnp.sum(jnp.where(hit, gram, 0.0), axis=0, keepdims=True)
    is_pos = row_id == lane_id + QD
    sbuf[v, NEG : NEG + 1, :] = jnp.sum(jnp.where(is_pos, gram, 0.0), axis=0, keepdims=True)
    sbuf[v, NEG + 1 :, :] = jnp.zeros((16 - NEG - 1, n_rows), jnp.float32)
    for i in range(1, 2 * NX):
        go(sbuf.at[v], vsend.at[i - 1], vrecv.at[i - 1], {"vocab": rem(v + i, 2 * NX)})
    for i in range(1, 2 * NX):
        ref = sbuf.at[rem(v + 2 * NX - i, 2 * NX)]
        remote(ref, ref, vsend.at[i - 1], vrecv.at[i - 1], {"vocab": rem(v + i, 2 * NX)}).wait_recv()
    total = sbuf[0]
    for i in range(1, 2 * NX):
        total = total + sbuf[i]
    lane8 = lax.broadcasted_iota(jnp.int32, (NEG, n_rows), 1)
    teacher_t = pltpu.roll(meta_t[0:NEG, :], n_rows - QD, 1)
    margin = total[NEG : NEG + 1, :] - total[0:NEG, :] - teacher_t
    margin = jnp.where(rem(lane8, 8) < QD, margin, 0.0)
    mt_ref[...] = jnp.concatenate([margin, jnp.zeros((120, n_rows), jnp.float32)], axis=0).T
    base = pl.multiple_of((z * NY + y) * 8, 8)
    m_loc = mt_ref[pl.ds(base, 8), :]
    margin_ref[...] = m_loc[0:QD, 0:NEG]

    meta_loc = rall[z, y, :, META:]
    sub_id = (lax.broadcasted_iota(jnp.int32, (8, n_rows), 0) + base).astype(jnp.float32)
    lanes = lax.broadcasted_iota(jnp.int32, (8, n_rows), 1).astype(jnp.float32)
    grad_pos_t = jnp.sum(margin, axis=0, keepdims=True)
    grad_pos_l = jnp.sum(m_loc[:, 0:NEG], axis=1, keepdims=True)
    coef = jnp.where(sub_id == lanes + QD, grad_pos_t, 0.0)
    coef = coef + jnp.where(lanes == sub_id + QD, grad_pos_l, 0.0)
    for k in range(NEG):
        coef = coef - jnp.where(sub_id == meta_t[k : k + 1, :], margin[k : k + 1, :], 0.0)
        coef = coef - jnp.where(lanes == meta_loc[:, k : k + 1], m_loc[:, k : k + 1], 0.0)
    rep_grad = lax.dot_general(
        coef, reps, (((1,), (0,)), ((), ())), precision=HI, preferred_element_type=jnp.float32
    )
    row0 = 0
    for g in range(2 * QD):
        span = LQ if g < QD else LP
        e = lg_f[row0 : row0 + span, :]
        lgrad[row0 : row0 + span, :] = ((e * inv_ref[g : g + 1, :]) * rep_grad[g : g + 1, :]).astype(jnp.bfloat16)
        row0 += span

    other = 1 - c

    def on_copy(n):
        return remote(psum_part.at[n, other], ron.at[n], osend.at[n], orecv.at[n], v_dev(x, other))

    def far_copy(n, way):
        return remote(
            fs.at[n, way], fr.at[n, way], fsend.at[n, way], frecv.at[n, way], v_dev((x_up, x_dn)[way], c)
        )

    def near_copy(n, way):
        return remote(
            ns.at[n, way], nr.at[n, way], nsend.at[n, way], nrecv.at[n, way], v_dev((x_up, x_dn)[way], c)
        )

    hw = CH // 2

    def bwd_body(n, carry):
        @pl.when(n < NCH)
        def _():
            rhs = jnp.concatenate([wt[n * (CH // KB) + i] for i in range(CH // KB)], axis=1)
            res = jnp.dot(lgrad[...], rhs, preferred_element_type=jnp.float32)
            for i in range(2 * NX):
                psum_part[n, i % 2, i // 2] = res[i * ROWS : (i + 1) * ROWS, :]
            on_copy(n).start()

        @pl.when((n >= S2) & (n < NCH + S2))
        def _():
            m = n - S2
            on_copy(m).wait_recv()
            far = psum_part[m, c, x_far] + ron[m, x_far]
            fs[m, 0] = far[:, :hw].astype(jnp.bfloat16)
            fs[m, 1] = far[:, hw:].astype(jnp.bfloat16)
            far_copy(m, 0).start()
            far_copy(m, 1).start()

        @pl.when((n >= S3) & (n < NCH + S3))
        def _():
            m = n - S3
            up = psum_part[m, c, x_up] + ron[m, x_up]
            dn = psum_part[m, c, x_dn] + ron[m, x_dn]
            far_copy(m, 0).wait_recv()
            far_copy(m, 1).wait_recv()
            ns[m, 0, :, :hw] = (up[:, :hw] + fr[m, 0].astype(jnp.float32)).astype(jnp.bfloat16)
            ns[m, 0, :, hw:] = up[:, hw:].astype(jnp.bfloat16)
            ns[m, 1, :, :hw] = dn[:, :hw].astype(jnp.bfloat16)
            ns[m, 1, :, hw:] = (dn[:, hw:] + fr[m, 1].astype(jnp.float32)).astype(jnp.bfloat16)
            near_copy(m, 0).start()
            near_copy(m, 1).start()

        @pl.when(n >= S4)
        def _():
            m = n - S4
            own = psum_part[m, c, x] + ron[m, x]
            near_copy(m, 0).wait_recv()
            near_copy(m, 1).wait_recv()
            cols = pl.ds(pl.multiple_of(m * CH, CH), CH)
            out_ref[:, cols] = own + nr[m, 0].astype(jnp.float32) + nr[m, 1].astype(jnp.float32)

        return carry

    lax.fori_loop(0, NCH + S4, bwd_body, 0)

    for cp in sends:
        cp.wait_send()

    for q in range(STREAMS):
        for sub in range(SUB):
            steps = FAR if sub in far_subs(q) else FAR - 1
            sent = wt.at[0:steps, 0 : sub_rows(q, sub), :]
            remote(sent, sent, rsend.at[q, sub], rrecv.at[q, 0, sub], nxt[q]).wait_send()
    for n in range(NCH):
        on_copy(n).wait_send()
        for way in range(2):
            far_copy(n, way).wait_send()
            near_copy(n, way).wait_send()


def per_device(
    hidden, head_weight, head_bias, query_len, passage_len, neg_owner, neg_index, teacher
):
    dma = pltpu.SemaphoreType.DMA
    vm = pltpu.VMEM
    f32, bf16 = jnp.float32, jnp.bfloat16
    margin, grad = pl.pallas_call(
        kernel,
        out_shape=(
            jax.ShapeDtypeStruct((QD, NEG), f32),
            jax.ShapeDtypeStruct((ROWS, D), f32),
        ),
        in_specs=[
            pl.BlockSpec(memory_space=pl.ANY),
            pl.BlockSpec(memory_space=pl.ANY),
            pl.BlockSpec(memory_space=pltpu.VMEM),
            pl.BlockSpec(memory_space=pltpu.SMEM),
            pl.BlockSpec(memory_space=pltpu.SMEM),
            pl.BlockSpec(memory_space=pltpu.VMEM),
            pl.BlockSpec(memory_space=pltpu.VMEM),
            pl.BlockSpec(memory_space=pltpu.VMEM),
        ],
        out_specs=(pl.BlockSpec(memory_space=pltpu.VMEM), pl.BlockSpec(memory_space=pltpu.VMEM)),
        scratch_shapes=[
            vm((NDP, VP, KB), bf16),
            vm((TOK, D), bf16),
            vm((1, VP), f32),
            vm((TOK, VP), f32),
            vm((NZ, NY, 8, RW), f32),
            vm((8, VP), f32),
            vm((TOK, VP), bf16),
            vm((2 * NX, 16, NDP * 8), f32),
            vm((NDP * 8, 128), f32),
            vm((NCH, 2, NX, ROWS, CH), f32),
            vm((NCH, NX, ROWS, CH), f32),
            vm((NCH, 2, ROWS, CH // 2), bf16),
            vm((NCH, 2, ROWS, CH // 2), bf16),
            vm((NCH, 2, ROWS, CH), bf16),
            vm((NCH, 2, ROWS, CH), bf16),
            dma((2,)),
            dma((STREAMS, SUB)),
            dma((STREAMS, FAR, SUB)),
            dma((NY + 1, 2, NZ // 2)),
            dma((NY + 1, 2, NZ // 2)),
            dma((NZ + 1, 3)),
            dma((NZ + 1, 3)),
            dma((2 * NX - 1,)),
            dma((2 * NX - 1,)),
            dma((NCH,)),
            dma((NCH,)),
            dma((NCH, 2)),
            dma((NCH, 2)),
            dma((NCH, 2)),
            dma((NCH, 2)),
        ],
        compiler_params=pltpu.CompilerParams(
            collective_id=0, has_side_effects=True, vmem_limit_bytes=60 * 1024 * 1024
        ),
    )(
        head_weight.T, hidden, head_bias[None, :], query_len, passage_len, neg_owner, neg_index, teacher
    )
    return margin, grad


def solution(mesh):
    return jax.shard_map(
        per_device,
        mesh=mesh,
        in_specs=(
            P("dp", None),
            P("dp", "vocab"),
            P("vocab"),
            P("dp"),
            P("dp"),
            P("dp", None),
            P("dp", None),
            P("dp", None),
        ),
        out_specs=(P("dp", None), P(("dp", "vocab"), None)),
        check_vma=False,
    )
```

```python
import functools

import jax
import jax.numpy as jnp
from jax import lax
from jax.experimental import pallas as pl
from jax.experimental.pallas import tpu as pltpu
from jax.sharding import PartitionSpec as P

NY, NZ, NX = 4, 8, 4
NDP = NY * NZ
LQ, LP, QD, NEG = 32, 64, 4, 8
TOK = QD * (LQ + LP)
D = 4096
KB = D // NDP
VW = 2000
VP = 2048
STREAMS = 4
CW = VP // STREAMS
HW = VP // 2
SUB = 4
SR = HW // SUB
FAR = NDP // 2
META = VP
RW = VP + 128
CH = 512
NCH = D // CH
S2, S3, S4 = 2, 5, 8
ROWS = TOK // 8
SCALE = 2.0**-64
TAU = 0.05
HI = lax.Precision.HIGHEST


def rem(a, n):
    return lax.rem(a, jnp.int32(n))


def div(a, n):
    return lax.div(a, jnp.int32(n))


def kernel(
    w_hbm, hid_hbm, bias_hbm, qlen_hbm, plen_hbm, owner_hbm, index_hbm, teacher_hbm,
    margin_ref, out_ref,
    wt, hid, bias_ref, qlen_ref, plen_ref, owner_ref, index_ref, teacher_ref, bias_s, lg_f, rall, inv_ref, lgrad, rhi, rlo, sbuf, mt_ref, psum_part, ron, fs, fr, ns, nr,
    ld_sem, rsend, rrecv, zsend, zrecv, ysend, yrecv, vsend, vrecv, osend, orecv, fsend, frecv, nsend, nrecv,
):
    dp = lax.axis_index("dp")
    v = lax.axis_index("vocab")
    y, z = div(dp, NZ), rem(dp, NZ)
    x, c = div(v, 2), rem(v, 2)
    y_up, y_dn = rem(y + 1, NY), rem(y + NY - 1, NY)
    z_up, z_dn = rem(z + 1, NZ), rem(z + NZ - 1, NZ)
    x_up, x_dn, x_far = rem(x + 1, NX), rem(x + NX - 1, NX), rem(x + 2, NX)

    def dp_dev(yy, zz):
        return {"dp": yy * NZ + zz}

    def v_dev(xx, cc):
        return {"vocab": xx * 2 + cc}

    def remote(src, dst, ss, rs, dev):
        return pltpu.make_async_remote_copy(
            src_ref=src, dst_ref=dst, send_sem=ss, recv_sem=rs, device_id=dev,
            device_id_type=pl.DeviceIdType.MESH,
        )

    ld_w = pltpu.make_async_copy(w_hbm, wt.at[dp, 0:VW, :], ld_sem.at[0])
    ld_h = pltpu.make_async_copy(hid_hbm, hid, ld_sem.at[1])
    ld_w.start()
    ld_h.start()
    small = [
        pltpu.make_async_copy(src, dst, ld_sem.at[2 + i])
        for i, (src, dst) in enumerate(
            [
                (bias_hbm, bias_ref), (qlen_hbm, qlen_ref), (plen_hbm, plen_ref),
                (owner_hbm, owner_ref), (index_hbm, index_ref), (teacher_hbm, teacher_ref),
            ]
        )
    ]
    for cp in small:
        cp.start()

    barrier = pltpu.get_barrier_semaphore()
    peers = [dp_dev(y_up, z), dp_dev(y_dn, z), dp_dev(y, z_up), dp_dev(y, z_dn)]
    peers += [{"vocab": rem(v + i, 2 * NX)} for i in range(1, 2 * NX)]
    for dev in peers:
        pl.semaphore_signal(barrier, inc=1, device_id=dev, device_id_type=pl.DeviceIdType.MESH)
    ld_w.wait()
    pl.semaphore_wait(barrier, len(peers))

    pos_a = NY * z + rem(y + z, NY)
    tb = rem(z + NY * NZ - (NY - 1) * y, NZ)
    pos_b = NY * (y + NY * div(tb, NY)) + rem(tb, NY)

    def at_a(p):
        b, i = div(p, NY), rem(p, NY)
        return rem(i + NY * NZ - b, NY) * NZ + b

    def at_b(p):
        b, i = div(p, NY), rem(p, NY)
        return rem(b, NY) * NZ + rem((NY - 1) * b + i, NZ)

    pos, at = (pos_a, pos_a, pos_b, pos_b), (at_a, at_a, at_b, at_b)
    sign = (1, -1, 1, -1)
    nxt = [{"dp": at[q](rem(pos[q] + NDP + sign[q], NDP))} for q in range(STREAMS)]

    def origin(q, s):
        return at[q](rem(pos[q] + 2 * NDP - sign[q] * s, NDP))

    def ring_copy(q, org, s, sub):
        part = wt.at[org, pl.ds((q // 2) * HW + sub * SR, sub_rows(q, sub)), :]
        return remote(part, part, rsend.at[q, sub], rrecv.at[q, s, sub], nxt[q])

    def sub_rows(q, sub):
        return SR if q < 2 or sub < SUB - 1 else VW - (VP - SR)

    def far_subs(q):
        return range(0, SUB // 2) if q % 2 == 0 else range(SUB // 2, SUB)

    for sub in range(SUB):
        for q in range(STREAMS):
            ring_copy(q, dp, 0, sub).start()

    def clear(i, carry):
        wt[i, VW:, :] = jnp.zeros((VP - VW, KB), jnp.bfloat16)
        return carry

    lax.fori_loop(0, NDP, clear, 0)
    for cp in small:
        cp.wait()
    bias_s[...] = jnp.zeros_like(bias_s)
    bias_s[:, 0:VW] = bias_ref[...]
    lg_f[...] = jnp.broadcast_to(bias_s[...], (TOK, VP))
    owner = owner_ref[...]
    ids = (rem(owner, NZ) * NY + div(owner, NZ)) * 8 + QD + index_ref[...]
    rall[z, y, :, META:] = jnp.zeros((8, 128), jnp.float32)
    rall[z, y, 0:QD, META : META + NEG] = ids.astype(jnp.float32)
    rall[z, y, QD:8, META : META + NEG] = teacher_ref[...]
    ld_h.wait()

    def mm(q, o1, o2):
        cols = slice(q * CW, (q + 1) * CW)
        k1 = pl.ds(pl.multiple_of(o1 * KB, KB), KB)
        k2 = pl.ds(pl.multiple_of(o2 * KB, KB), KB)
        rhs = jnp.concatenate([wt[o1, cols, :], wt[o2, cols, :]], axis=1)
        lhs = jnp.concatenate([hid[:, k1], hid[:, k2]], axis=1)
        lg_f[:, cols] += lax.dot_general(
            lhs, rhs, (((1,), (1,)), ((), ())), preferred_element_type=jnp.float32
        )

    def mm_after(sub, org):
        mm(sub, org[sub // 2 * 2], org[sub // 2 * 2 + 1])

    def ring_body(s, before):
        org = [origin(q, s) for q in range(STREAMS)]
        for sub in range(SUB):
            for q in range(STREAMS):
                ring_copy(q, org[q], s - 1, sub).wait_recv()
                if sub in far_subs(q):
                    ring_copy(q, org[q], s, sub).start()
                else:

                    @pl.when(s < FAR - 1)
                    def _():
                        ring_copy(q, org[q], s, sub).start()

            @pl.when(s > 1)
            def _():
                mm_after(sub, before)

        return tuple(org)

    before = lax.fori_loop(1, FAR, ring_body, (dp,) * STREAMS)
    for sub in range(SUB):
        mm_after(sub, before)
    for q in range(STREAMS):
        for sub in far_subs(q):
            ring_copy(q, origin(q, FAR), FAR - 1, sub).wait_recv()
    for q in range(STREAMS):
        mm(q, dp, origin(q // 2 * 2, FAR))

    row0 = 0
    for g in range(2 * QD):
        span = LQ if g < QD else LP
        n = qlen_ref[g] if g < QD else plen_ref[g - QD]
        mask = lax.broadcasted_iota(jnp.int32, (span, CW), 0) < n
        count = n.astype(jnp.float32)
        for q in range(STREAMS):
            cols = slice(q * CW, (q + 1) * CW)
            l = lg_f[row0 : row0 + span, cols]
            u = 1.0 + jnp.maximum(l, 0.0)
            u2 = u * u
            u4 = u2 * u2
            u8 = u4 * u4
            u16 = u8 * u8
            u19 = jnp.where(mask, u16 * (u2 * u), 0.0)
            summed = jnp.sum(u19 * u, axis=0, keepdims=True)
            lg_f[row0 : row0 + span, cols] = jnp.where(l > 0.0, u19 * SCALE, 0.0)
            rall[z, y, g : g + 1, cols] = TAU * jnp.log(summed / count)
            inv_ref[g : g + 1, cols] = 1.0 / (summed * SCALE)
        row0 += span

    half = VP // 2
    h1 = pl.ds(0, half)
    h0 = pl.ds(half, RW - half)
    far1 = (pl.ds(0, half // 2), pl.ds(half // 2, half // 2))
    far0 = (pl.ds(half, 512), pl.ds(half + 512, RW - half - 512))
    sends = []

    def go(src, ss, rs, dev):
        cp = remote(src, src, ss, rs, dev)
        cp.start()
        sends.append(cp)

    z_next = (dp_dev(y, z_up), dp_dev(y, z_dn))
    y_off = [y, y_dn, y_up, rem(y + 2, NY)]
    mid = NZ // 2

    def z_origin(way, d):
        return rem(z + NZ - d, NZ) if way == 0 else rem(z + d, NZ)

    def z_copy(j, way, d, zo):
        if j < NY:
            ref = rall.at[zo, y_off[j], :, far0[way] if d == mid else h0]
        else:
            ref = rall.at[zo, y, :, far1[way] if d == mid else h1]
        return remote(ref, ref, zsend.at[j, way, d - 1], zrecv.at[j, way, d - 1], z_next[way])

    def z_send(j, way, d):
        cp = z_copy(j, way, d, z_origin(way, d - 1))
        cp.start()
        sends.append(cp)

    def z_wait(j, way, d):
        z_copy(j, way, d, z_origin(way, d)).wait_recv()

    def y_send(slot, zo, cols):
        go(rall.at[zo, y, :, cols], ysend.at[slot, 0], yrecv.at[slot, 0], dp_dev(y_up, z))
        go(rall.at[zo, y, :, cols], ysend.at[slot, 1], yrecv.at[slot, 1], dp_dev(y_dn, z))
        go(rall.at[zo, y, :, cols], ysend.at[slot, 2], yrecv.at[slot, 2], dp_dev(rem(y + 2, NY), z))

    def y_wait(slot, way, zo, cols):
        ref = rall.at[zo, y_off[way + 1], :, cols]
        remote(ref, ref, ysend.at[slot, way], yrecv.at[slot, way], dp_dev(y_up, z)).wait_recv()

    y_send(NZ, z, h0)
    for way in range(2):
        z_send(NY, way, 1)
        z_send(0, way, 1)
    y_send(0, z, h1)
    for j in range(1, NY):
        y_wait(NZ, j - 1, z, h0)
        for way in range(2):
            z_send(j, way, 1)
    order = [(0, z)]
    for d in range(1, mid + 1):
        for j in (NY, 0, 1, 2, 3):
            for way in range(2):
                z_wait(j, way, d)
                if d < mid:
                    z_send(j, way, d + 1)
                if j == NY and (d < mid or way == 1):
                    slot = 2 * d - 1 + way if d < mid else NZ - 1
                    y_send(slot, z_origin(way, d), h1)
                    order.append((slot, z_origin(way, d)))
    for slot, zo in order:
        for way in range(3):
            y_wait(slot, way, zo, h1)

    n_rows = NDP * 8
    reps = rall[:, :, :, 0:VP].reshape(n_rows, VP)
    high = reps.astype(jnp.bfloat16)
    rhi[...] = high
    rlo[...] = (reps - high.astype(jnp.float32)).astype(jnp.bfloat16)

    def nt(p, q):
        return lax.dot_general(p, q, (((1,), (1,)), ((), ())), preferred_element_type=jnp.float32)

    gram = nt(rhi[...], rhi[...]) + (nt(rhi[...], rlo[...]) + nt(rlo[...], rhi[...]))
    meta = rall[:, :, :, META:].reshape(n_rows, 128)
    meta_t = meta.T
    row_id = lax.broadcasted_iota(jnp.int32, (n_rows, n_rows), 0).astype(jnp.float32)
    lane_id = lax.broadcasted_iota(jnp.int32, (n_rows, n_rows), 1).astype(jnp.float32)
    for k in range(NEG):
        hit = row_id == meta_t[k : k + 1, :]
        sbuf[v, k : k + 1, :] = jnp.sum(jnp.where(hit, gram, 0.0), axis=0, keepdims=True)
    is_pos = row_id == lane_id + QD
    sbuf[v, NEG : NEG + 1, :] = jnp.sum(jnp.where(is_pos, gram, 0.0), axis=0, keepdims=True)
    sbuf[v, NEG + 1 :, :] = jnp.zeros((16 - NEG - 1, n_rows), jnp.float32)
    for i in range(1, 2 * NX):
        go(sbuf.at[v], vsend.at[i - 1], vrecv.at[i - 1], {"vocab": rem(v + i, 2 * NX)})
    for i in range(1, 2 * NX):
        ref = sbuf.at[rem(v + 2 * NX - i, 2 * NX)]
        remote(ref, ref, vsend.at[i - 1], vrecv.at[i - 1], {"vocab": rem(v + i, 2 * NX)}).wait_recv()
    total = sbuf[0]
    for i in range(1, 2 * NX):
        total = total + sbuf[i]
    lane8 = lax.broadcasted_iota(jnp.int32, (NEG, n_rows), 1)
    teacher_t = pltpu.roll(meta_t[0:NEG, :], n_rows - QD, 1)
    margin = total[NEG : NEG + 1, :] - total[0:NEG, :] - teacher_t
    margin = jnp.where(rem(lane8, 8) < QD, margin, 0.0)
    mt_ref[...] = jnp.concatenate([margin, jnp.zeros((120, n_rows), jnp.float32)], axis=0).T
    base = pl.multiple_of((z * NY + y) * 8, 8)
    m_loc = mt_ref[pl.ds(base, 8), :]
    margin_ref[...] = m_loc[0:QD, 0:NEG]

    meta_loc = rall[z, y, :, META:]
    sub_id = (lax.broadcasted_iota(jnp.int32, (8, n_rows), 0) + base).astype(jnp.float32)
    lanes = lax.broadcasted_iota(jnp.int32, (8, n_rows), 1).astype(jnp.float32)
    grad_pos_t = jnp.sum(margin, axis=0, keepdims=True)
    grad_pos_l = jnp.sum(m_loc[:, 0:NEG], axis=1, keepdims=True)
    coef = jnp.where(sub_id == lanes + QD, grad_pos_t, 0.0)
    coef = coef + jnp.where(lanes == sub_id + QD, grad_pos_l, 0.0)
    for k in range(NEG):
        coef = coef - jnp.where(sub_id == meta_t[k : k + 1, :], margin[k : k + 1, :], 0.0)
        coef = coef - jnp.where(lanes == meta_loc[:, k : k + 1], m_loc[:, k : k + 1], 0.0)
    coef_hi = coef.astype(jnp.bfloat16).astype(jnp.float32)
    both = jnp.concatenate([coef_hi, coef - coef_hi], axis=0).astype(jnp.bfloat16)
    by_hi = jnp.dot(both, rhi[...], preferred_element_type=jnp.float32)
    by_lo = jnp.dot(both, rlo[...], preferred_element_type=jnp.float32)
    rep_grad = by_hi[0:8, :] + (by_hi[8:16, :] + by_lo[0:8, :])
    row0 = 0
    for g in range(2 * QD):
        span = LQ if g < QD else LP
        e = lg_f[row0 : row0 + span, :]
        lgrad[row0 : row0 + span, :] = ((e * inv_ref[g : g + 1, :]) * rep_grad[g : g + 1, :]).astype(jnp.bfloat16)
        row0 += span

    other = 1 - c

    def on_copy(n):
        return remote(psum_part.at[n, other], ron.at[n], osend.at[n], orecv.at[n], v_dev(x, other))

    def far_copy(n, way):
        return remote(
            fs.at[n, way], fr.at[n, way], fsend.at[n, way], frecv.at[n, way], v_dev((x_up, x_dn)[way], c)
        )

    def near_copy(n, way):
        return remote(
            ns.at[n, way], nr.at[n, way], nsend.at[n, way], nrecv.at[n, way], v_dev((x_up, x_dn)[way], c)
        )

    hw = CH // 2

    def bwd_body(n, carry):
        @pl.when(n < NCH)
        def _():
            rhs = jnp.concatenate([wt[n * (CH // KB) + i] for i in range(CH // KB)], axis=1)
            res = jnp.dot(lgrad[...], rhs, preferred_element_type=jnp.float32)
            for i in range(2 * NX):
                psum_part[n, i % 2, i // 2] = res[i * ROWS : (i + 1) * ROWS, :]
            on_copy(n).start()

        @pl.when((n >= S2) & (n < NCH + S2))
        def _():
            m = n - S2
            on_copy(m).wait_recv()
            far = psum_part[m, c, x_far] + ron[m, x_far]
            fs[m, 0] = far[:, :hw].astype(jnp.bfloat16)
            fs[m, 1] = far[:, hw:].astype(jnp.bfloat16)
            far_copy(m, 0).start()
            far_copy(m, 1).start()

        @pl.when((n >= S3) & (n < NCH + S3))
        def _():
            m = n - S3
            up = psum_part[m, c, x_up] + ron[m, x_up]
            dn = psum_part[m, c, x_dn] + ron[m, x_dn]
            far_copy(m, 0).wait_recv()
            far_copy(m, 1).wait_recv()
            ns[m, 0, :, :hw] = (up[:, :hw] + fr[m, 0].astype(jnp.float32)).astype(jnp.bfloat16)
            ns[m, 0, :, hw:] = up[:, hw:].astype(jnp.bfloat16)
            ns[m, 1, :, :hw] = dn[:, :hw].astype(jnp.bfloat16)
            ns[m, 1, :, hw:] = (dn[:, hw:] + fr[m, 1].astype(jnp.float32)).astype(jnp.bfloat16)
            near_copy(m, 0).start()
            near_copy(m, 1).start()

        @pl.when(n >= S4)
        def _():
            m = n - S4
            own = psum_part[m, c, x] + ron[m, x]
            near_copy(m, 0).wait_recv()
            near_copy(m, 1).wait_recv()
            cols = pl.ds(pl.multiple_of(m * CH, CH), CH)
            out_ref[:, cols] = own + nr[m, 0].astype(jnp.float32) + nr[m, 1].astype(jnp.float32)

        return carry

    lax.fori_loop(0, NCH + S4, bwd_body, 0)

    for cp in sends:
        cp.wait_send()

    for q in range(STREAMS):
        for sub in range(SUB):
            steps = FAR if sub in far_subs(q) else FAR - 1
            sent = wt.at[0:steps, 0 : sub_rows(q, sub), :]
            remote(sent, sent, rsend.at[q, sub], rrecv.at[q, 0, sub], nxt[q]).wait_send()
    for n in range(NCH):
        on_copy(n).wait_send()
        for way in range(2):
            far_copy(n, way).wait_send()
            near_copy(n, way).wait_send()


def per_device(
    hidden, head_weight, head_bias, query_len, passage_len, neg_owner, neg_index, teacher
):
    dma = pltpu.SemaphoreType.DMA
    vm = pltpu.VMEM
    f32, bf16 = jnp.float32, jnp.bfloat16
    margin, grad = pl.pallas_call(
        kernel,
        out_shape=(
            jax.ShapeDtypeStruct((QD, NEG), f32),
            jax.ShapeDtypeStruct((ROWS, D), f32),
        ),
        in_specs=[pl.BlockSpec(memory_space=pl.ANY)] * 8,
        out_specs=(pl.BlockSpec(memory_space=pltpu.VMEM), pl.BlockSpec(memory_space=pltpu.VMEM)),
        scratch_shapes=[
            vm((NDP, VP, KB), bf16),
            vm((TOK, D), bf16),
            vm((1, VW), f32),
            pltpu.SMEM((QD,), jnp.int32),
            pltpu.SMEM((QD,), jnp.int32),
            vm((QD, NEG), jnp.int32),
            vm((QD, NEG), jnp.int32),
            vm((QD, NEG), f32),
            vm((1, VP), f32),
            vm((TOK, VP), f32),
            vm((NZ, NY, 8, RW), f32),
            vm((8, VP), f32),
            vm((TOK, VP), bf16),
            vm((NDP * 8, VP), bf16),
            vm((NDP * 8, VP), bf16),
            vm((2 * NX, 16, NDP * 8), f32),
            vm((NDP * 8, 128), f32),
            vm((NCH, 2, NX, ROWS, CH), f32),
            vm((NCH, NX, ROWS, CH), f32),
            vm((NCH, 2, ROWS, CH // 2), bf16),
            vm((NCH, 2, ROWS, CH // 2), bf16),
            vm((NCH, 2, ROWS, CH), bf16),
            vm((NCH, 2, ROWS, CH), bf16),
            dma((8,)),
            dma((STREAMS, SUB)),
            dma((STREAMS, FAR, SUB)),
            dma((NY + 1, 2, NZ // 2)),
            dma((NY + 1, 2, NZ // 2)),
            dma((NZ + 1, 3)),
            dma((NZ + 1, 3)),
            dma((2 * NX - 1,)),
            dma((2 * NX - 1,)),
            dma((NCH,)),
            dma((NCH,)),
            dma((NCH, 2)),
            dma((NCH, 2)),
            dma((NCH, 2)),
            dma((NCH, 2)),
        ],
        compiler_params=pltpu.CompilerParams(
            collective_id=0, has_side_effects=True, vmem_limit_bytes=60 * 1024 * 1024
        ),
    )(
        head_weight.T, hidden, head_bias[None, :], query_len, passage_len, neg_owner, neg_index, teacher
    )
    return margin, grad


def solution(mesh):
    return jax.shard_map(
        per_device,
        mesh=mesh,
        in_specs=(
            P("dp", None),
            P("dp", "vocab"),
            P("vocab"),
            P("dp"),
            P("dp"),
            P("dp", None),
            P("dp", None),
            P("dp", None),
        ),
        out_specs=(P("dp", None), P(("dp", "vocab"), None)),
        check_vma=False,
    )
```

```python
import functools

import jax
import jax.numpy as jnp
from jax import lax
from jax.experimental import pallas as pl
from jax.experimental.pallas import tpu as pltpu
from jax.sharding import PartitionSpec as P

NY, NZ, NX = 4, 8, 4
NDP = NY * NZ
LQ, LP, QD, NEG = 32, 64, 4, 8
TOK = QD * (LQ + LP)
D = 4096
KB = D // NDP
VW = 2000
VP = 2048
STREAMS = 4
CW = VP // STREAMS
HW = VP // 2
SUB = 2
PER = STREAMS // SUB
SR = HW // SUB
FAR = NDP // 2
META = VP
RW = VP + 128
CH = 512
NCH = D // CH
S2, S3, S4 = 2, 5, 8
ROWS = TOK // 8
SCALE = 2.0**-64
TAU = 0.05
HI = lax.Precision.HIGHEST


def rem(a, n):
    return lax.rem(a, jnp.int32(n))


def div(a, n):
    return lax.div(a, jnp.int32(n))


def kernel(
    w_hbm, hid_hbm, bias_hbm, qlen_hbm, plen_hbm, owner_hbm, index_hbm, teacher_hbm,
    margin_ref, out_ref,
    wt, hid, bias_ref, qlen_ref, plen_ref, owner_ref, index_ref, teacher_ref, bias_s, lg_f, rall, inv_ref, lgrad, rhi, rlo, sbuf, mt_ref, psum_part, ron, fs, fr, ns, nr,
    ld_sem, rsend, rrecv, zsend, zrecv, ysend, yrecv, vsend, vrecv, osend, orecv, fsend, frecv, nsend, nrecv,
):
    dp = lax.axis_index("dp")
    v = lax.axis_index("vocab")
    y, z = div(dp, NZ), rem(dp, NZ)
    x, c = div(v, 2), rem(v, 2)
    y_up, y_dn = rem(y + 1, NY), rem(y + NY - 1, NY)
    z_up, z_dn = rem(z + 1, NZ), rem(z + NZ - 1, NZ)
    x_up, x_dn, x_far = rem(x + 1, NX), rem(x + NX - 1, NX), rem(x + 2, NX)

    def dp_dev(yy, zz):
        return {"dp": yy * NZ + zz}

    def v_dev(xx, cc):
        return {"vocab": xx * 2 + cc}

    def remote(src, dst, ss, rs, dev):
        return pltpu.make_async_remote_copy(
            src_ref=src, dst_ref=dst, send_sem=ss, recv_sem=rs, device_id=dev,
            device_id_type=pl.DeviceIdType.MESH,
        )

    ld_w = pltpu.make_async_copy(w_hbm, wt.at[dp, 0:VW, :], ld_sem.at[0])
    ld_h = pltpu.make_async_copy(hid_hbm, hid, ld_sem.at[1])
    ld_w.start()
    ld_h.start()
    small = [
        pltpu.make_async_copy(src, dst, ld_sem.at[2 + i])
        for i, (src, dst) in enumerate(
            [
                (bias_hbm, bias_ref), (qlen_hbm, qlen_ref), (plen_hbm, plen_ref),
                (owner_hbm, owner_ref), (index_hbm, index_ref), (teacher_hbm, teacher_ref),
            ]
        )
    ]
    for cp in small:
        cp.start()

    barrier = pltpu.get_barrier_semaphore()
    peers = [dp_dev(y_up, z), dp_dev(y_dn, z), dp_dev(y, z_up), dp_dev(y, z_dn)]
    peers += [{"vocab": rem(v + i, 2 * NX)} for i in range(1, 2 * NX)]
    for dev in peers:
        pl.semaphore_signal(barrier, inc=1, device_id=dev, device_id_type=pl.DeviceIdType.MESH)
    ld_w.wait()
    pl.semaphore_wait(barrier, len(peers))

    pos_a = NY * z + rem(y + z, NY)
    tb = rem(z + NY * NZ - (NY - 1) * y, NZ)
    pos_b = NY * (y + NY * div(tb, NY)) + rem(tb, NY)

    def at_a(p):
        b, i = div(p, NY), rem(p, NY)
        return rem(i + NY * NZ - b, NY) * NZ + b

    def at_b(p):
        b, i = div(p, NY), rem(p, NY)
        return rem(b, NY) * NZ + rem((NY - 1) * b + i, NZ)

    pos, at = (pos_a, pos_a, pos_b, pos_b), (at_a, at_a, at_b, at_b)
    sign = (1, -1, 1, -1)
    nxt = [{"dp": at[q](rem(pos[q] + NDP + sign[q], NDP))} for q in range(STREAMS)]

    def origin(q, s):
        return at[q](rem(pos[q] + 2 * NDP - sign[q] * s, NDP))

    def ring_copy(q, org, s, sub):
        part = wt.at[org, pl.ds((q // 2) * HW + sub * SR, sub_rows(q, sub)), :]
        return remote(part, part, rsend.at[q, sub], rrecv.at[q, s, sub], nxt[q])

    def sub_rows(q, sub):
        return SR if q < 2 or sub < SUB - 1 else VW - (VP - SR)

    def far_subs(q):
        return range(0, SUB // 2) if q % 2 == 0 else range(SUB // 2, SUB)

    for sub in range(SUB):
        for q in range(STREAMS):
            ring_copy(q, dp, 0, sub).start()

    def clear(i, carry):
        wt[i, VW:, :] = jnp.zeros((VP - VW, KB), jnp.bfloat16)
        return carry

    lax.fori_loop(0, NDP, clear, 0)
    for cp in small:
        cp.wait()
    bias_s[...] = jnp.zeros_like(bias_s)
    bias_s[:, 0:VW] = bias_ref[...]
    lg_f[...] = jnp.broadcast_to(bias_s[...], (TOK, VP))
    owner = owner_ref[...]
    ids = (rem(owner, NZ) * NY + div(owner, NZ)) * 8 + QD + index_ref[...]
    rall[z, y, :, META:] = jnp.zeros((8, 128), jnp.float32)
    rall[z, y, 0:QD, META : META + NEG] = ids.astype(jnp.float32)
    rall[z, y, QD:8, META : META + NEG] = teacher_ref[...]
    ld_h.wait()

    def mm(q, o1, o2):
        cols = slice(q * CW, (q + 1) * CW)
        k1 = pl.ds(pl.multiple_of(o1 * KB, KB), KB)
        k2 = pl.ds(pl.multiple_of(o2 * KB, KB), KB)
        rhs = jnp.concatenate([wt[o1, cols, :], wt[o2, cols, :]], axis=1)
        lhs = jnp.concatenate([hid[:, k1], hid[:, k2]], axis=1)
        lg_f[:, cols] += lax.dot_general(
            lhs, rhs, (((1,), (1,)), ((), ())), preferred_element_type=jnp.float32
        )

    def mm_after(sub, org):
        mm(sub, org[sub // 2 * 2], org[sub // 2 * 2 + 1])

    def ring_body(s, before):
        org = [origin(q, s) for q in range(STREAMS)]
        for sub in range(SUB):
            for q in range(STREAMS):
                ring_copy(q, org[q], s - 1, sub).wait_recv()
                if sub in far_subs(q):
                    ring_copy(q, org[q], s, sub).start()
                else:

                    @pl.when(s < FAR - 1)
                    def _():
                        ring_copy(q, org[q], s, sub).start()

            @pl.when(s > 1)
            def _():
                for i in range(PER):
                    mm_after(sub * PER + i, before)

        return tuple(org)

    before = lax.fori_loop(1, FAR, ring_body, (dp,) * STREAMS)
    for sub in range(STREAMS):
        mm_after(sub, before)
    for q in range(STREAMS):
        for sub in far_subs(q):
            ring_copy(q, origin(q, FAR), FAR - 1, sub).wait_recv()
    for q in range(STREAMS):
        mm(q, dp, origin(q // 2 * 2, FAR))

    row0 = 0
    for g in range(2 * QD):
        span = LQ if g < QD else LP
        n = qlen_ref[g] if g < QD else plen_ref[g - QD]
        mask = lax.broadcasted_iota(jnp.int32, (span, CW), 0) < n
        count = n.astype(jnp.float32)
        for q in range(STREAMS):
            cols = slice(q * CW, (q + 1) * CW)
            l = lg_f[row0 : row0 + span, cols]
            u = 1.0 + jnp.maximum(l, 0.0)
            u2 = u * u
            u4 = u2 * u2
            u8 = u4 * u4
            u16 = u8 * u8
            u19 = jnp.where(mask, u16 * (u2 * u), 0.0)
            summed = jnp.sum(u19 * u, axis=0, keepdims=True)
            lg_f[row0 : row0 + span, cols] = jnp.where(l > 0.0, u19 * SCALE, 0.0)
            rall[z, y, g : g + 1, cols] = TAU * jnp.log(summed / count)
            inv_ref[g : g + 1, cols] = 1.0 / (summed * SCALE)
        row0 += span

    half = VP // 2
    h1 = pl.ds(0, half)
    h0 = pl.ds(half, RW - half)
    far1 = (pl.ds(0, half // 2), pl.ds(half // 2, half // 2))
    far0 = (pl.ds(half, 512), pl.ds(half + 512, RW - half - 512))

    def go(src, ss, rs, dev):
        remote(src, src, ss, rs, dev).start()

    z_next = (dp_dev(y, z_up), dp_dev(y, z_dn))
    y_off = [y, y_dn, y_up, rem(y + 2, NY)]
    mid = NZ // 2

    def z_origin(way, d):
        return rem(z + NZ - d, NZ) if way == 0 else rem(z + d, NZ)

    def z_copy(j, way, d, zo):
        if j < NY:
            ref = rall.at[zo, y_off[j], :, far0[way] if d == mid else h0]
        else:
            ref = rall.at[zo, y, :, far1[way] if d == mid else h1]
        return remote(ref, ref, zsend.at[j // NY], zrecv.at[j, way, d - 1], z_next[way])

    def z_send(j, way, d):
        z_copy(j, way, d, z_origin(way, d - 1)).start()

    def z_wait(j, way, d):
        z_copy(j, way, d, z_origin(way, d)).wait_recv()

    def y_send(slot, zo, cols):
        go(rall.at[zo, y, :, cols], ysend.at[slot // NZ], yrecv.at[slot, 0], dp_dev(y_up, z))
        go(rall.at[zo, y, :, cols], ysend.at[slot // NZ], yrecv.at[slot, 1], dp_dev(y_dn, z))
        go(rall.at[zo, y, :, cols], ysend.at[slot // NZ], yrecv.at[slot, 2], dp_dev(rem(y + 2, NY), z))

    def y_wait(slot, way, zo, cols):
        ref = rall.at[zo, y_off[way + 1], :, cols]
        remote(ref, ref, ysend.at[slot // NZ], yrecv.at[slot, way], dp_dev(y_up, z)).wait_recv()

    y_send(NZ, z, h0)
    for way in range(2):
        z_send(NY, way, 1)
        z_send(0, way, 1)
    y_send(0, z, h1)
    for j in range(1, NY):
        y_wait(NZ, j - 1, z, h0)
        for way in range(2):
            z_send(j, way, 1)
    order = [(0, z)]
    for d in range(1, mid + 1):
        for j in (NY, 0, 1, 2, 3):
            for way in range(2):
                z_wait(j, way, d)
                if d < mid:
                    z_send(j, way, d + 1)
                if j == NY and (d < mid or way == 1):
                    slot = 2 * d - 1 + way if d < mid else NZ - 1
                    y_send(slot, z_origin(way, d), h1)
                    order.append((slot, z_origin(way, d)))
    for slot, zo in order:
        for way in range(3):
            y_wait(slot, way, zo, h1)

    n_rows = NDP * 8
    reps = rall[:, :, :, 0:VP].reshape(n_rows, VP)
    high = reps.astype(jnp.bfloat16)
    rhi[...] = high
    rlo[...] = (reps - high.astype(jnp.float32)).astype(jnp.bfloat16)

    def nt(p, q):
        return lax.dot_general(p, q, (((1,), (1,)), ((), ())), preferred_element_type=jnp.float32)

    gram = nt(rhi[...], rhi[...]) + (nt(rhi[...], rlo[...]) + nt(rlo[...], rhi[...]))
    meta = rall[:, :, :, META:].reshape(n_rows, 128)
    meta_t = meta.T
    row_id = lax.broadcasted_iota(jnp.int32, (n_rows, n_rows), 0).astype(jnp.float32)
    lane_id = lax.broadcasted_iota(jnp.int32, (n_rows, n_rows), 1).astype(jnp.float32)
    for k in range(NEG):
        hit = row_id == meta_t[k : k + 1, :]
        sbuf[v, k : k + 1, :] = jnp.sum(jnp.where(hit, gram, 0.0), axis=0, keepdims=True)
    is_pos = row_id == lane_id + QD
    sbuf[v, NEG : NEG + 1, :] = jnp.sum(jnp.where(is_pos, gram, 0.0), axis=0, keepdims=True)
    sbuf[v, NEG + 1 :, :] = jnp.zeros((16 - NEG - 1, n_rows), jnp.float32)
    for i in range(1, 2 * NX):
        go(sbuf.at[v], vsend.at[0], vrecv.at[i - 1], {"vocab": rem(v + i, 2 * NX)})
    for i in range(1, 2 * NX):
        ref = sbuf.at[rem(v + 2 * NX - i, 2 * NX)]
        remote(ref, ref, vsend.at[0], vrecv.at[i - 1], {"vocab": rem(v + i, 2 * NX)}).wait_recv()
    total = sbuf[0]
    for i in range(1, 2 * NX):
        total = total + sbuf[i]
    lane8 = lax.broadcasted_iota(jnp.int32, (NEG, n_rows), 1)
    teacher_t = pltpu.roll(meta_t[0:NEG, :], n_rows - QD, 1)
    margin = total[NEG : NEG + 1, :] - total[0:NEG, :] - teacher_t
    margin = jnp.where(rem(lane8, 8) < QD, margin, 0.0)
    mt_ref[...] = jnp.concatenate([margin, jnp.zeros((120, n_rows), jnp.float32)], axis=0).T
    base = pl.multiple_of((z * NY + y) * 8, 8)
    m_loc = mt_ref[pl.ds(base, 8), :]
    margin_ref[...] = m_loc[0:QD, 0:NEG]

    meta_loc = rall[z, y, :, META:]
    sub_id = (lax.broadcasted_iota(jnp.int32, (8, n_rows), 0) + base).astype(jnp.float32)
    lanes = lax.broadcasted_iota(jnp.int32, (8, n_rows), 1).astype(jnp.float32)
    grad_pos_t = jnp.sum(margin, axis=0, keepdims=True)
    grad_pos_l = jnp.sum(m_loc[:, 0:NEG], axis=1, keepdims=True)
    coef = jnp.where(sub_id == lanes + QD, grad_pos_t, 0.0)
    coef = coef + jnp.where(lanes == sub_id + QD, grad_pos_l, 0.0)
    for k in range(NEG):
        coef = coef - jnp.where(sub_id == meta_t[k : k + 1, :], margin[k : k + 1, :], 0.0)
        coef = coef - jnp.where(lanes == meta_loc[:, k : k + 1], m_loc[:, k : k + 1], 0.0)
    coef_hi = coef.astype(jnp.bfloat16).astype(jnp.float32)
    both = jnp.concatenate([coef_hi, coef - coef_hi], axis=0).astype(jnp.bfloat16)
    by_hi = jnp.dot(both, rhi[...], preferred_element_type=jnp.float32)
    by_lo = jnp.dot(both, rlo[...], preferred_element_type=jnp.float32)
    rep_grad = by_hi[0:8, :] + (by_hi[8:16, :] + by_lo[0:8, :])
    row0 = 0
    for g in range(2 * QD):
        span = LQ if g < QD else LP
        e = lg_f[row0 : row0 + span, :]
        lgrad[row0 : row0 + span, :] = ((e * inv_ref[g : g + 1, :]) * rep_grad[g : g + 1, :]).astype(jnp.bfloat16)
        row0 += span

    other = 1 - c

    def on_copy(n):
        return remote(psum_part.at[n, other], ron.at[n], osend.at[0], orecv.at[n], v_dev(x, other))

    def far_copy(n, way):
        return remote(
            fs.at[n, way], fr.at[n, way], fsend.at[0], frecv.at[n, way], v_dev((x_up, x_dn)[way], c)
        )

    def near_copy(n, way):
        return remote(
            ns.at[n, way], nr.at[n, way], nsend.at[0], nrecv.at[n, way], v_dev((x_up, x_dn)[way], c)
        )

    hw = CH // 2

    def bwd_body(n, carry):
        @pl.when(n < NCH)
        def _():
            rhs = jnp.concatenate([wt[n * (CH // KB) + i] for i in range(CH // KB)], axis=1)
            res = jnp.dot(lgrad[...], rhs, preferred_element_type=jnp.float32)
            for i in range(2 * NX):
                psum_part[n, i % 2, i // 2] = res[i * ROWS : (i + 1) * ROWS, :]
            on_copy(n).start()

        @pl.when((n >= S2) & (n < NCH + S2))
        def _():
            m = n - S2
            on_copy(m).wait_recv()
            far = psum_part[m, c, x_far] + ron[m, x_far]
            fs[m, 0] = far[:, :hw].astype(jnp.bfloat16)
            fs[m, 1] = far[:, hw:].astype(jnp.bfloat16)
            far_copy(m, 0).start()
            far_copy(m, 1).start()

        @pl.when((n >= S3) & (n < NCH + S3))
        def _():
            m = n - S3
            up = psum_part[m, c, x_up] + ron[m, x_up]
            dn = psum_part[m, c, x_dn] + ron[m, x_dn]
            far_copy(m, 0).wait_recv()
            far_copy(m, 1).wait_recv()
            ns[m, 0, :, :hw] = (up[:, :hw] + fr[m, 0].astype(jnp.float32)).astype(jnp.bfloat16)
            ns[m, 0, :, hw:] = up[:, hw:].astype(jnp.bfloat16)
            ns[m, 1, :, :hw] = dn[:, :hw].astype(jnp.bfloat16)
            ns[m, 1, :, hw:] = (dn[:, hw:] + fr[m, 1].astype(jnp.float32)).astype(jnp.bfloat16)
            near_copy(m, 0).start()
            near_copy(m, 1).start()

        @pl.when(n >= S4)
        def _():
            m = n - S4
            own = psum_part[m, c, x] + ron[m, x]
            near_copy(m, 0).wait_recv()
            near_copy(m, 1).wait_recv()
            cols = pl.ds(pl.multiple_of(m * CH, CH), CH)
            out_ref[:, cols] = own + nr[m, 0].astype(jnp.float32) + nr[m, 1].astype(jnp.float32)

        return carry

    lax.fori_loop(0, NCH + S4, bwd_body, 0)

    def sent_all(ref, ss, rs):
        remote(ref, ref, ss, rs, v_dev(x, other)).wait_send()

    sent_all(rall.at[0 : NZ - 1, :, :, h0], zsend.at[0], zrecv.at[0, 0, 0])
    sent_all(rall.at[0 : NZ - 1, 0, :, h1], zsend.at[1], zrecv.at[0, 0, 0])
    sent_all(rall.at[0 : 3 * NZ // NY, :, :, h1], ysend.at[0], yrecv.at[0, 0])
    sent_all(rall.at[0, 0:3, :, h0], ysend.at[1], yrecv.at[0, 0])
    sent_all(sbuf.at[0 : 2 * NX - 1], vsend.at[0], vrecv.at[0])
    sent_all(ron, osend.at[0], orecv.at[0])
    sent_all(fs, fsend.at[0], frecv.at[0, 0])
    sent_all(ns, nsend.at[0], nrecv.at[0, 0])

    for q in range(STREAMS):
        for sub in range(SUB):
            steps = FAR if sub in far_subs(q) else FAR - 1
            sent = wt.at[0:steps, 0 : sub_rows(q, sub), :]
            remote(sent, sent, rsend.at[q, sub], rrecv.at[q, 0, sub], nxt[q]).wait_send()


def per_device(
    hidden, head_weight, head_bias, query_len, passage_len, neg_owner, neg_index, teacher
):
    dma = pltpu.SemaphoreType.DMA
    vm = pltpu.VMEM
    f32, bf16 = jnp.float32, jnp.bfloat16
    margin, grad = pl.pallas_call(
        kernel,
        out_shape=(
            jax.ShapeDtypeStruct((QD, NEG), f32),
            jax.ShapeDtypeStruct((ROWS, D), f32),
        ),
        in_specs=[pl.BlockSpec(memory_space=pl.ANY)] * 8,
        out_specs=(pl.BlockSpec(memory_space=pltpu.VMEM), pl.BlockSpec(memory_space=pltpu.VMEM)),
        scratch_shapes=[
            vm((NDP, VP, KB), bf16),
            vm((TOK, D), bf16),
            vm((1, VW), f32),
            pltpu.SMEM((QD,), jnp.int32),
            pltpu.SMEM((QD,), jnp.int32),
            vm((QD, NEG), jnp.int32),
            vm((QD, NEG), jnp.int32),
            vm((QD, NEG), f32),
            vm((1, VP), f32),
            vm((TOK, VP), f32),
            vm((NZ, NY, 8, RW), f32),
            vm((8, VP), f32),
            vm((TOK, VP), bf16),
            vm((NDP * 8, VP), bf16),
            vm((NDP * 8, VP), bf16),
            vm((2 * NX, 16, NDP * 8), f32),
            vm((NDP * 8, 128), f32),
            vm((NCH, 2, NX, ROWS, CH), f32),
            vm((NCH, NX, ROWS, CH), f32),
            vm((NCH, 2, ROWS, CH // 2), bf16),
            vm((NCH, 2, ROWS, CH // 2), bf16),
            vm((NCH, 2, ROWS, CH), bf16),
            vm((NCH, 2, ROWS, CH), bf16),
            dma((8,)),
            dma((STREAMS, SUB)),
            dma((STREAMS, FAR, SUB)),
            dma((2,)),
            dma((NY + 1, 2, NZ // 2)),
            dma((2,)),
            dma((NZ + 1, 3)),
            dma((1,)),
            dma((2 * NX - 1,)),
            dma((1,)),
            dma((NCH,)),
            dma((1,)),
            dma((NCH, 2)),
            dma((1,)),
            dma((NCH, 2)),
        ],
        compiler_params=pltpu.CompilerParams(
            collective_id=0, has_side_effects=True, vmem_limit_bytes=60 * 1024 * 1024
        ),
    )(
        head_weight.T, hidden, head_bias[None, :], query_len, passage_len, neg_owner, neg_index, teacher
    )
    return margin, grad


def solution(mesh):
    return jax.shard_map(
        per_device,
        mesh=mesh,
        in_specs=(
            P("dp", None),
            P("dp", "vocab"),
            P("vocab"),
            P("dp"),
            P("dp"),
            P("dp", None),
            P("dp", None),
            P("dp", None),
        ),
        out_specs=(P("dp", None), P(("dp", "vocab"), None)),
        check_vma=False,
    )
```

```python
import functools

import jax
import jax.numpy as jnp
from jax import lax
from jax.experimental import pallas as pl
from jax.experimental.pallas import tpu as pltpu
from jax.sharding import PartitionSpec as P

NY, NZ, NX = 4, 8, 4
NDP = NY * NZ
LQ, LP, QD, NEG = 32, 64, 4, 8
TOK = QD * (LQ + LP)
D = 4096
KB = D // NDP
VW = 2000
VP = 2048
STREAMS = 4
CW = VP // STREAMS
HW = VP // 2
SUB = 2
PER = STREAMS // SUB
SR = HW // SUB
FAR = NDP // 2
META = VP
RW = VP + 128
CH = 512
NCH = D // CH
S2, S3, S4 = 2, 5, 8
ROWS = TOK // 8
SCALE = 2.0**-64
TAU = 0.05
HI = lax.Precision.HIGHEST


def rem(a, n):
    return lax.rem(a, jnp.int32(n))


def div(a, n):
    return lax.div(a, jnp.int32(n))


def kernel(
    w_hbm, hid_hbm, bias_hbm, qlen_hbm, plen_hbm, owner_hbm, index_hbm, teacher_hbm,
    margin_ref, out_hbm,
    wt, out_s, hid, bias_ref, qlen_ref, plen_ref, owner_ref, index_ref, teacher_ref, bias_s, lg_f, rall, inv_ref, lgrad, rhi, rlo, sbuf, mt_ref, psum_part, ron, fs, fr, ns, nr,
    ld_sem, rsend, rrecv, zsend, zrecv, ysend, yrecv, vsend, vrecv, osend, orecv, fsend, frecv, nsend, nrecv,
):
    dp = lax.axis_index("dp")
    v = lax.axis_index("vocab")
    y, z = div(dp, NZ), rem(dp, NZ)
    x, c = div(v, 2), rem(v, 2)
    y_up, y_dn = rem(y + 1, NY), rem(y + NY - 1, NY)
    z_up, z_dn = rem(z + 1, NZ), rem(z + NZ - 1, NZ)
    x_up, x_dn, x_far = rem(x + 1, NX), rem(x + NX - 1, NX), rem(x + 2, NX)

    def dp_dev(yy, zz):
        return {"dp": yy * NZ + zz}

    def v_dev(xx, cc):
        return {"vocab": xx * 2 + cc}

    def remote(src, dst, ss, rs, dev):
        return pltpu.make_async_remote_copy(
            src_ref=src, dst_ref=dst, send_sem=ss, recv_sem=rs, device_id=dev,
            device_id_type=pl.DeviceIdType.MESH,
        )

    ld_w = pltpu.make_async_copy(w_hbm, wt.at[dp, 0:VW, :], ld_sem.at[0])
    ld_h = pltpu.make_async_copy(hid_hbm, hid, ld_sem.at[1])
    ld_w.start()
    ld_h.start()
    small = [
        pltpu.make_async_copy(src, dst, ld_sem.at[2 + i])
        for i, (src, dst) in enumerate(
            [
                (bias_hbm, bias_ref), (qlen_hbm, qlen_ref), (plen_hbm, plen_ref),
                (owner_hbm, owner_ref), (index_hbm, index_ref), (teacher_hbm, teacher_ref),
            ]
        )
    ]
    for cp in small:
        cp.start()

    barrier = pltpu.get_barrier_semaphore()
    peers = [dp_dev(y_up, z), dp_dev(y_dn, z), dp_dev(y, z_up), dp_dev(y, z_dn)]
    peers += [{"vocab": rem(v + i, 2 * NX)} for i in range(1, 2 * NX)]
    for dev in peers:
        pl.semaphore_signal(barrier, inc=1, device_id=dev, device_id_type=pl.DeviceIdType.MESH)
    ld_w.wait()
    pl.semaphore_wait(barrier, len(peers))

    pos_a = NY * z + rem(y + z, NY)
    tb = rem(z + NY * NZ - (NY - 1) * y, NZ)
    pos_b = NY * (y + NY * div(tb, NY)) + rem(tb, NY)

    def at_a(p):
        b, i = div(p, NY), rem(p, NY)
        return rem(i + NY * NZ - b, NY) * NZ + b

    def at_b(p):
        b, i = div(p, NY), rem(p, NY)
        return rem(b, NY) * NZ + rem((NY - 1) * b + i, NZ)

    pos, at = (pos_a, pos_a, pos_b, pos_b), (at_a, at_a, at_b, at_b)
    sign = (1, -1, 1, -1)
    nxt = [{"dp": at[q](rem(pos[q] + NDP + sign[q], NDP))} for q in range(STREAMS)]

    def origin(q, s):
        return at[q](rem(pos[q] + 2 * NDP - sign[q] * s, NDP))

    def ring_copy(q, org, s, sub):
        part = wt.at[org, pl.ds((q // 2) * HW + sub * SR, sub_rows(q, sub)), :]
        return remote(part, part, rsend.at[q, sub], rrecv.at[q, s, sub], nxt[q])

    def sub_rows(q, sub):
        return SR if q < 2 or sub < SUB - 1 else VW - (VP - SR)

    def far_subs(q):
        return range(0, SUB // 2) if q % 2 == 0 else range(SUB // 2, SUB)

    for sub in range(SUB):
        for q in range(STREAMS):
            ring_copy(q, dp, 0, sub).start()

    def clear(i, carry):
        wt[i, VW:, :] = jnp.zeros((VP - VW, KB), jnp.bfloat16)
        return carry

    lax.fori_loop(0, NDP, clear, 0)
    for cp in small:
        cp.wait()
    bias_s[...] = jnp.zeros_like(bias_s)
    bias_s[:, 0:VW] = bias_ref[...]
    lg_f[...] = jnp.broadcast_to(bias_s[...], (TOK, VP))
    owner = owner_ref[...]
    ids = (rem(owner, NZ) * NY + div(owner, NZ)) * 8 + QD + index_ref[...]
    rall[z, y, :, META:] = jnp.zeros((8, 128), jnp.float32)
    rall[z, y, 0:QD, META : META + NEG] = ids.astype(jnp.float32)
    rall[z, y, QD:8, META : META + NEG] = teacher_ref[...]
    ld_h.wait()

    def mm(q, o1, o2):
        cols = slice(q * CW, (q + 1) * CW)
        k1 = pl.ds(pl.multiple_of(o1 * KB, KB), KB)
        k2 = pl.ds(pl.multiple_of(o2 * KB, KB), KB)
        rhs = jnp.concatenate([wt[o1, cols, :], wt[o2, cols, :]], axis=1)
        lhs = jnp.concatenate([hid[:, k1], hid[:, k2]], axis=1)
        lg_f[:, cols] += lax.dot_general(
            lhs, rhs, (((1,), (1,)), ((), ())), preferred_element_type=jnp.float32
        )

    def mm_after(sub, org):
        mm(sub, org[sub // 2 * 2], org[sub // 2 * 2 + 1])

    def ring_body(s, before):
        org = [origin(q, s) for q in range(STREAMS)]
        for sub in range(SUB):
            for q in range(STREAMS):
                ring_copy(q, org[q], s - 1, sub).wait_recv()
                if sub in far_subs(q):
                    ring_copy(q, org[q], s, sub).start()
                else:

                    @pl.when(s < FAR - 1)
                    def _():
                        ring_copy(q, org[q], s, sub).start()

            @pl.when(s > 1)
            def _():
                for i in range(PER):
                    mm_after(sub * PER + i, before)

        return tuple(org)

    before = lax.fori_loop(1, FAR, ring_body, (dp,) * STREAMS)
    for sub in range(STREAMS):
        mm_after(sub, before)
    for q in range(STREAMS):
        for sub in far_subs(q):
            ring_copy(q, origin(q, FAR), FAR - 1, sub).wait_recv()
    for q in range(STREAMS):
        mm(q, dp, origin(q // 2 * 2, FAR))

    row0 = 0
    for g in range(2 * QD):
        span = LQ if g < QD else LP
        n = qlen_ref[g] if g < QD else plen_ref[g - QD]
        mask = lax.broadcasted_iota(jnp.int32, (span, CW), 0) < n
        count = n.astype(jnp.float32)
        for q in range(STREAMS):
            cols = slice(q * CW, (q + 1) * CW)
            l = lg_f[row0 : row0 + span, cols]
            u = 1.0 + jnp.maximum(l, 0.0)
            u2 = u * u
            u4 = u2 * u2
            u8 = u4 * u4
            u16 = u8 * u8
            u19 = jnp.where(mask, u16 * (u2 * u), 0.0)
            summed = jnp.sum(u19 * u, axis=0, keepdims=True)
            lg_f[row0 : row0 + span, cols] = jnp.where(l > 0.0, u19 * SCALE, 0.0)
            rall[z, y, g : g + 1, cols] = TAU * jnp.log(summed / count)
            inv_ref[g : g + 1, cols] = 1.0 / (summed * SCALE)
        row0 += span

    half = VP // 2
    h1 = pl.ds(0, half)
    h0 = pl.ds(half, RW - half)
    far1 = (pl.ds(0, half // 2), pl.ds(half // 2, half // 2))
    far0 = (pl.ds(half, 512), pl.ds(half + 512, RW - half - 512))

    def go(src, ss, rs, dev):
        remote(src, src, ss, rs, dev).start()

    z_next = (dp_dev(y, z_up), dp_dev(y, z_dn))
    y_off = [y, y_dn, y_up, rem(y + 2, NY)]
    mid = NZ // 2

    def z_origin(way, d):
        return rem(z + NZ - d, NZ) if way == 0 else rem(z + d, NZ)

    def z_copy(j, way, d, zo):
        if j < NY:
            ref = rall.at[zo, y_off[j], :, far0[way] if d == mid else h0]
        else:
            ref = rall.at[zo, y, :, far1[way] if d == mid else h1]
        return remote(ref, ref, zsend.at[j // NY], zrecv.at[j, way, d - 1], z_next[way])

    def z_send(j, way, d):
        z_copy(j, way, d, z_origin(way, d - 1)).start()

    def z_wait(j, way, d):
        z_copy(j, way, d, z_origin(way, d)).wait_recv()

    def y_send(slot, zo, cols):
        go(rall.at[zo, y, :, cols], ysend.at[slot // NZ], yrecv.at[slot, 0], dp_dev(y_up, z))
        go(rall.at[zo, y, :, cols], ysend.at[slot // NZ], yrecv.at[slot, 1], dp_dev(y_dn, z))
        go(rall.at[zo, y, :, cols], ysend.at[slot // NZ], yrecv.at[slot, 2], dp_dev(rem(y + 2, NY), z))

    def y_wait(slot, way, zo, cols):
        ref = rall.at[zo, y_off[way + 1], :, cols]
        remote(ref, ref, ysend.at[slot // NZ], yrecv.at[slot, way], dp_dev(y_up, z)).wait_recv()

    y_send(NZ, z, h0)
    for way in range(2):
        z_send(NY, way, 1)
        z_send(0, way, 1)
    y_send(0, z, h1)
    for j in range(1, NY):
        y_wait(NZ, j - 1, z, h0)
        for way in range(2):
            z_send(j, way, 1)
    order = [(0, z)]
    for d in range(1, mid + 1):
        for j in (NY, 0, 1, 2, 3):
            for way in range(2):
                z_wait(j, way, d)
                if d < mid:
                    z_send(j, way, d + 1)
                if j == NY and (d < mid or way == 1):
                    slot = 2 * d - 1 + way if d < mid else NZ - 1
                    y_send(slot, z_origin(way, d), h1)
                    order.append((slot, z_origin(way, d)))
    for slot, zo in order:
        for way in range(3):
            y_wait(slot, way, zo, h1)

    n_rows = NDP * 8
    reps = rall[:, :, :, 0:VP].reshape(n_rows, VP)
    high = reps.astype(jnp.bfloat16)
    rhi[...] = high
    rlo[...] = (reps - high.astype(jnp.float32)).astype(jnp.bfloat16)

    def nt(p, q):
        return lax.dot_general(p, q, (((1,), (1,)), ((), ())), preferred_element_type=jnp.float32)

    gram = nt(rhi[...], rhi[...]) + (nt(rhi[...], rlo[...]) + nt(rlo[...], rhi[...]))
    meta = rall[:, :, :, META:].reshape(n_rows, 128)
    meta_t = meta.T
    row_id = lax.broadcasted_iota(jnp.int32, (n_rows, n_rows), 0).astype(jnp.float32)
    lane_id = lax.broadcasted_iota(jnp.int32, (n_rows, n_rows), 1).astype(jnp.float32)
    for k in range(NEG):
        hit = row_id == meta_t[k : k + 1, :]
        sbuf[v, k : k + 1, :] = jnp.sum(jnp.where(hit, gram, 0.0), axis=0, keepdims=True)
    is_pos = row_id == lane_id + QD
    sbuf[v, NEG : NEG + 1, :] = jnp.sum(jnp.where(is_pos, gram, 0.0), axis=0, keepdims=True)
    sbuf[v, NEG + 1 :, :] = jnp.zeros((16 - NEG - 1, n_rows), jnp.float32)
    for i in range(1, 2 * NX):
        go(sbuf.at[v], vsend.at[0], vrecv.at[i - 1], {"vocab": rem(v + i, 2 * NX)})
    for i in range(1, 2 * NX):
        ref = sbuf.at[rem(v + 2 * NX - i, 2 * NX)]
        remote(ref, ref, vsend.at[0], vrecv.at[i - 1], {"vocab": rem(v + i, 2 * NX)}).wait_recv()
    total = sbuf[0]
    for i in range(1, 2 * NX):
        total = total + sbuf[i]
    lane8 = lax.broadcasted_iota(jnp.int32, (NEG, n_rows), 1)
    teacher_t = pltpu.roll(meta_t[0:NEG, :], n_rows - QD, 1)
    margin = total[NEG : NEG + 1, :] - total[0:NEG, :] - teacher_t
    margin = jnp.where(rem(lane8, 8) < QD, margin, 0.0)
    mt_ref[...] = jnp.concatenate([margin, jnp.zeros((120, n_rows), jnp.float32)], axis=0).T
    base = pl.multiple_of((z * NY + y) * 8, 8)
    m_loc = mt_ref[pl.ds(base, 8), :]
    margin_ref[...] = m_loc[0:QD, 0:NEG]

    meta_loc = rall[z, y, :, META:]
    sub_id = (lax.broadcasted_iota(jnp.int32, (8, n_rows), 0) + base).astype(jnp.float32)
    lanes = lax.broadcasted_iota(jnp.int32, (8, n_rows), 1).astype(jnp.float32)
    grad_pos_t = jnp.sum(margin, axis=0, keepdims=True)
    grad_pos_l = jnp.sum(m_loc[:, 0:NEG], axis=1, keepdims=True)
    coef = jnp.where(sub_id == lanes + QD, grad_pos_t, 0.0)
    coef = coef + jnp.where(lanes == sub_id + QD, grad_pos_l, 0.0)
    for k in range(NEG):
        coef = coef - jnp.where(sub_id == meta_t[k : k + 1, :], margin[k : k + 1, :], 0.0)
        coef = coef - jnp.where(lanes == meta_loc[:, k : k + 1], m_loc[:, k : k + 1], 0.0)
    coef_hi = coef.astype(jnp.bfloat16).astype(jnp.float32)
    both = jnp.concatenate([coef_hi, coef - coef_hi], axis=0).astype(jnp.bfloat16)
    by_hi = jnp.dot(both, rhi[...], preferred_element_type=jnp.float32)
    by_lo = jnp.dot(both, rlo[...], preferred_element_type=jnp.float32)
    rep_grad = by_hi[0:8, :] + (by_hi[8:16, :] + by_lo[0:8, :])
    row0 = 0
    for g in range(2 * QD):
        span = LQ if g < QD else LP
        e = lg_f[row0 : row0 + span, :]
        lgrad[row0 : row0 + span, :] = ((e * inv_ref[g : g + 1, :]) * rep_grad[g : g + 1, :]).astype(jnp.bfloat16)
        row0 += span

    other = 1 - c

    def on_copy(n):
        return remote(psum_part.at[n, other], ron.at[n], osend.at[0], orecv.at[n], v_dev(x, other))

    def far_copy(n, way):
        return remote(
            fs.at[n, way], fr.at[n, way], fsend.at[0], frecv.at[n, way], v_dev((x_up, x_dn)[way], c)
        )

    def near_copy(n, way):
        return remote(
            ns.at[n, way], nr.at[n, way], nsend.at[0], nrecv.at[n, way], v_dev((x_up, x_dn)[way], c)
        )

    hw = CH // 2

    def bwd_body(n, carry):
        @pl.when(n < NCH)
        def _():
            rhs = jnp.concatenate([wt[n * (CH // KB) + i] for i in range(CH // KB)], axis=1)
            res = jnp.dot(lgrad[...], rhs, preferred_element_type=jnp.float32)
            for i in range(2 * NX):
                psum_part[n, i % 2, i // 2] = res[i * ROWS : (i + 1) * ROWS, :]
            on_copy(n).start()

        @pl.when((n >= S2) & (n < NCH + S2))
        def _():
            m = n - S2
            on_copy(m).wait_recv()
            far = psum_part[m, c, x_far] + ron[m, x_far]
            fs[m, 0] = far[:, :hw].astype(jnp.bfloat16)
            fs[m, 1] = far[:, hw:].astype(jnp.bfloat16)
            far_copy(m, 0).start()
            far_copy(m, 1).start()

        @pl.when((n >= S3) & (n < NCH + S3))
        def _():
            m = n - S3
            up = psum_part[m, c, x_up] + ron[m, x_up]
            dn = psum_part[m, c, x_dn] + ron[m, x_dn]
            far_copy(m, 0).wait_recv()
            far_copy(m, 1).wait_recv()
            ns[m, 0, :, :hw] = (up[:, :hw] + fr[m, 0].astype(jnp.float32)).astype(jnp.bfloat16)
            ns[m, 0, :, hw:] = up[:, hw:].astype(jnp.bfloat16)
            ns[m, 1, :, :hw] = dn[:, :hw].astype(jnp.bfloat16)
            ns[m, 1, :, hw:] = (dn[:, hw:] + fr[m, 1].astype(jnp.float32)).astype(jnp.bfloat16)
            near_copy(m, 0).start()
            near_copy(m, 1).start()

        @pl.when(n >= S4)
        def _():
            m = n - S4
            own = psum_part[m, c, x] + ron[m, x]
            near_copy(m, 0).wait_recv()
            near_copy(m, 1).wait_recv()
            cols = pl.ds(pl.multiple_of(m * CH, CH), CH)
            out_s[:, cols] = own + nr[m, 0].astype(jnp.float32) + nr[m, 1].astype(jnp.float32)
            pltpu.make_async_copy(out_s.at[:, cols], out_hbm.at[:, cols], ld_sem.at[8]).start()

        return carry

    lax.fori_loop(0, NCH + S4, bwd_body, 0)

    pltpu.make_async_copy(out_s, out_hbm, ld_sem.at[8]).wait()
    def sent_all(ref, ss, rs):
        remote(ref, ref, ss, rs, v_dev(x, other)).wait_send()

    sent_all(rall.at[0 : NZ - 1, :, :, h0], zsend.at[0], zrecv.at[0, 0, 0])
    sent_all(rall.at[0 : NZ - 1, 0, :, h1], zsend.at[1], zrecv.at[0, 0, 0])
    sent_all(rall.at[0 : 3 * NZ // NY, :, :, h1], ysend.at[0], yrecv.at[0, 0])
    sent_all(rall.at[0, 0:3, :, h0], ysend.at[1], yrecv.at[0, 0])
    sent_all(sbuf.at[0 : 2 * NX - 1], vsend.at[0], vrecv.at[0])
    sent_all(ron, osend.at[0], orecv.at[0])
    sent_all(fs, fsend.at[0], frecv.at[0, 0])
    sent_all(ns, nsend.at[0], nrecv.at[0, 0])

    for q in range(STREAMS):
        for sub in range(SUB):
            steps = FAR if sub in far_subs(q) else FAR - 1
            sent = wt.at[0:steps, 0 : sub_rows(q, sub), :]
            remote(sent, sent, rsend.at[q, sub], rrecv.at[q, 0, sub], nxt[q]).wait_send()


def per_device(
    hidden, head_weight, head_bias, query_len, passage_len, neg_owner, neg_index, teacher
):
    dma = pltpu.SemaphoreType.DMA
    vm = pltpu.VMEM
    f32, bf16 = jnp.float32, jnp.bfloat16
    margin, grad = pl.pallas_call(
        kernel,
        out_shape=(
            jax.ShapeDtypeStruct((QD, NEG), f32),
            jax.ShapeDtypeStruct((ROWS, D), f32),
        ),
        in_specs=[pl.BlockSpec(memory_space=pl.ANY)] * 8,
        out_specs=(pl.BlockSpec(memory_space=pltpu.VMEM), pl.BlockSpec(memory_space=pl.ANY)),
        scratch_shapes=[
            vm((NDP, VP, KB), bf16),
            vm((ROWS, D), f32),
            vm((TOK, D), bf16),
            vm((1, VW), f32),
            pltpu.SMEM((QD,), jnp.int32),
            pltpu.SMEM((QD,), jnp.int32),
            vm((QD, NEG), jnp.int32),
            vm((QD, NEG), jnp.int32),
            vm((QD, NEG), f32),
            vm((1, VP), f32),
            vm((TOK, VP), f32),
            vm((NZ, NY, 8, RW), f32),
            vm((8, VP), f32),
            vm((TOK, VP), bf16),
            vm((NDP * 8, VP), bf16),
            vm((NDP * 8, VP), bf16),
            vm((2 * NX, 16, NDP * 8), f32),
            vm((NDP * 8, 128), f32),
            vm((NCH, 2, NX, ROWS, CH), f32),
            vm((NCH, NX, ROWS, CH), f32),
            vm((NCH, 2, ROWS, CH // 2), bf16),
            vm((NCH, 2, ROWS, CH // 2), bf16),
            vm((NCH, 2, ROWS, CH), bf16),
            vm((NCH, 2, ROWS, CH), bf16),
            dma((9,)),
            dma((STREAMS, SUB)),
            dma((STREAMS, FAR, SUB)),
            dma((2,)),
            dma((NY + 1, 2, NZ // 2)),
            dma((2,)),
            dma((NZ + 1, 3)),
            dma((1,)),
            dma((2 * NX - 1,)),
            dma((1,)),
            dma((NCH,)),
            dma((1,)),
            dma((NCH, 2)),
            dma((1,)),
            dma((NCH, 2)),
        ],
        compiler_params=pltpu.CompilerParams(
            collective_id=0, has_side_effects=True, vmem_limit_bytes=60 * 1024 * 1024
        ),
    )(
        head_weight.T, hidden, head_bias[None, :], query_len, passage_len, neg_owner, neg_index, teacher
    )
    return margin, grad


def solution(mesh):
    return jax.shard_map(
        per_device,
        mesh=mesh,
        in_specs=(
            P("dp", None),
            P("dp", "vocab"),
            P("vocab"),
            P("dp"),
            P("dp"),
            P("dp", None),
            P("dp", None),
            P("dp", None),
        ),
        out_specs=(P("dp", None), P(("dp", "vocab"), None)),
        check_vma=False,
    )
```
